32 devices in a mesh: row: 8 (over y, x, core), col: 4 (over z).
Axes of the slice: x: 2, y: 2, z: 4, core: 2. Of those that a mesh axis runs over, the one named last changes fastest.
Arguments:
- panel_u: bfloat16 [2, 8, 1024, 160], P(None, 'row', 'col'), may hold values from -6 to 6
- panel_v: bfloat16 [2, 8, 1024, 160], P(None, 'row', 'col'), may hold values from -0.0625 to 0.0625
- panel_rank: int32 [2, 8], P(None, 'row'), may hold values from 32 to 160, as said below
- diag_inverse: bfloat16 [1024, 1024], P('col'), as said below
- tile_u: bfloat16 [2, 8, 4, 1024, 160], P(None, 'row', 'col'), may hold values from -6 to 6
- tile_v: bfloat16 [2, 8, 4, 1024, 160], P(None, 'row', 'col'), may hold values from -0.5 to 0.5
- tile_rank: int32 [2, 8, 4], P(None, 'row', 'col'), may hold values from 32 to 160, as said below
- sketch: bfloat16 [2, 8, 4, 1024, 160], P(None, 'row', 'col'), may hold values from -6 to 6
Outputs:
- new_u: float32 [2, 8, 4, 1024, 160], P(None, 'row', 'col')
- new_v: float32 [2, 8, 4, 1024, 160], P(None, 'row', 'col')
The draws below stay inside these ranges and needn't reach their ends.
Inputs may be any that keep to these rules, and one draw needn't show every extreme that they name: `panel_rank`: some panel tile has rank 160. `tile_rank`: some trailing tile has rank 160. `diag_inverse`: lower triangular with diagonal entries of 1 to 2.
All inputs are finite; a program needn't handle non-finite values.
Results may differ from the reference program's by a relative error of at most 0.0037.
Values may be sent and summed in bfloat16 or wider, within the bound.
No kernel may reach another device: no remote copies, remote signals or barrier semaphores. Data moves between devices by JAX's collectives and lax.ppermute only.
A program may use at most 64 MiB of HBM per device.

```python
import math
import jax
import jax.numpy as jnp
from jax import lax

B = 1024
RMAX = 160
JC = 2
N_ROW = 8
N_COL = 4


def draw_diag_inverse(key, part):
    first, second = jax.random.split(key)
    lower_part = jax.random.normal(first, (B, B), jnp.float32) / jnp.sqrt(jnp.float32(B))
    rows = jnp.arange(B)[:, None]
    columns = jnp.arange(B)[None, :]
    middle = jax.random.uniform(second, (B,), jnp.float32, 1.0, 2.0)
    return (jnp.where(rows > columns, lower_part, 0.0) + jnp.where(rows == columns, middle[:, None], 0.0)).astype(jnp.bfloat16)


def ranks_with_top(key, shape, count):
    base = jax.random.randint(key, (count,), RMAX // 5, RMAX + 1)
    spot = jax.random.randint(jax.random.fold_in(key, 7), (), 0, count)
    base = jnp.where(jnp.arange(count) == spot, RMAX, base)
    return base.reshape(shape).astype(jnp.int32)


def draw_panel_rank(key, part):
    return ranks_with_top(key, (2, N_ROW), 2 * N_ROW)


def draw_tile_rank(key, part):
    return ranks_with_top(key, (JC, N_ROW, N_COL), JC * N_ROW * N_COL)


def shard_levels(own_key, extent, shards, smallest, high):
    def one(position, blocks):
        draws = jax.random.uniform(jax.random.fold_in(jax.random.fold_in(own_key, 6), position), (blocks,), jnp.float32, smallest / len(shards), high / len(shards))
        return jnp.repeat(jnp.exp(draws), extent[position] // blocks).reshape((-1,) + (1,) * (len(extent) - position - 1))

    loudness = one(*shards[0])
    for cut in shards[1:]:
        loudness = loudness * one(*cut)
    return loudness


def gaussian(rng, extent, deviation, bound, cuts=(), kind=jnp.bfloat16):
    result = jax.random.normal(rng, extent, jnp.float32) * deviation
    if len(cuts) > 0:
        result = shard_levels(rng, extent, cuts, -0.22, 0.18) * result
    return jnp.clip(result, min=-bound, max=bound).astype(kind)


def setup_inputs(seed: int = 0) -> dict:
    splits = jax.random.split(jax.random.key(seed), 9)
    return {
        "panel_u": gaussian(splits[0], (2, N_ROW, B, RMAX), 1.0, 6.0, ((1, 8), (2, 4))),
        "panel_v": gaussian(splits[1], (2, N_ROW, B, RMAX), (RMAX * B // 16) ** -0.5, 0.0625, ((1, 8), (2, 4))),
        "panel_rank": draw_panel_rank(jax.random.fold_in(splits[8], 71), 0),
        "diag_inverse": draw_diag_inverse(jax.random.fold_in(splits[8], 71), 0),
        "tile_u": gaussian(splits[4], (JC, N_ROW, N_COL, B, RMAX), 1.0, 6.0, ((1, 8), (2, 4))),
        "tile_v": gaussian(splits[5], (JC, N_ROW, N_COL, B, RMAX), RMAX ** -0.5, 0.5, ((1, 8), (2, 4))),
        "tile_rank": draw_tile_rank(jax.random.fold_in(splits[8], 71), 0),
        "sketch": gaussian(splits[7], (JC, N_ROW, N_COL, B, RMAX), 1.0, 6.0, ((1, 8), (2, 4))),
    }


def recompress(old_u, old_v, row_u, row_s, col_u, col_s, omega, rank):
    high = lax.Precision.HIGHEST
    width = old_u.shape[1]
    keep = (jnp.arange(width, dtype=jnp.int32) < rank).astype(jnp.float32)
    ou = old_u.astype(jnp.float32) * keep
    ov = old_v.astype(jnp.float32) * keep
    om = omega.astype(jnp.float32) * keep
    ru = row_u.astype(jnp.float32)
    rs = row_s.astype(jnp.float32)
    cu = col_u.astype(jnp.float32)
    cs = col_s.astype(jnp.float32)
    coupling = jnp.dot(rs.T, cs, precision=high)
    sketched = jnp.dot(ou, jnp.dot(ov.T, om, precision=high), precision=high)
    sketched = sketched - jnp.dot(ru, jnp.dot(coupling, jnp.dot(cu.T, om, precision=high), precision=high), precision=high)
    gram = jnp.dot(sketched.T, sketched, precision=high) + jnp.diag(1.0 - keep)
    lower = jnp.linalg.cholesky(gram)
    basis = lax.linalg.triangular_solve(lower, sketched, left_side=False, lower=True, transpose_a=True)
    factor = math.sqrt(old_u.shape[0])
    right = jnp.dot(ov, jnp.dot(ou.T, basis, precision=high), precision=high)
    right = right - jnp.dot(cu, jnp.dot(coupling.T, jnp.dot(ru.T, basis, precision=high), precision=high), precision=high)
    return (basis * factor, right / factor)

def reference(panel_u, panel_v, panel_rank, diag_inverse, tile_u, tile_v, tile_rank, sketch):
    width = panel_u.shape[3]
    keep = (jnp.arange(width, dtype=jnp.int32)[None, None, None, :] < panel_rank[:, :, None, None]).astype(jnp.bfloat16)
    masked_u = panel_u * keep
    masked_v = panel_v * keep
    solved = jnp.einsum('ab,tsbr->tsar', diag_inverse.astype(jnp.float32), masked_v.astype(jnp.float32), precision=lax.Precision.HIGHEST).astype(jnp.bfloat16)
    count = JC * N_ROW * N_COL
    flat_u = tile_u.reshape(count, B, width)
    flat_v = tile_v.reshape(count, B, width)
    flat_s = sketch.reshape(count, B, width)
    flat_r = tile_rank.reshape(count)
    indices = jnp.arange(count, dtype=jnp.int32)

    def one_tile(items):
        index, old_u, old_v, omega, rank = items
        prow = index // N_COL % N_ROW
        pcol = index // (N_ROW * N_COL) * N_COL + index % N_COL
        return recompress(old_u, old_v, masked_u[1, prow], solved[1, prow], masked_u[0, pcol], solved[0, pcol], omega, rank)
    out_u, out_v = lax.map(one_tile, (indices, flat_u, flat_v, flat_s, flat_r))
    shape = (JC, N_ROW, N_COL, B, width)
    return (out_u.reshape(shape), out_v.reshape(shape))
```

```python
import functools
import math

import jax
import jax.numpy as jnp
from jax import lax
from jax.experimental import pallas as pl
from jax.experimental.pallas import tpu as pltpu
from jax.sharding import PartitionSpec as P


F32 = jnp.float32
BF16 = jnp.bfloat16
HIGH = lax.Precision.HIGHEST
STEP = 32
VMEM = pl.BlockSpec(memory_space=pltpu.VMEM)
SMEM = pl.BlockSpec(memory_space=pltpu.SMEM)
ANY = pl.BlockSpec(memory_space=pl.ANY)


def contract(a, b, dims, precision=None):
    return lax.dot_general(
        a, b, (dims, ((), ())), preferred_element_type=F32, precision=precision
    )


NN = ((1,), (0,))
NT = ((1,), (1,))
TN = ((0,), (0,))


def parts(value, count=3):
    found = []
    for _ in range(count - 1):
        head = value.astype(BF16)
        found.append(head)
        value = value - head.astype(F32)
    found.append(value.astype(BF16))
    return found


def turned(value):
    return value.astype(F32).T


def mask_kernel(rank_ref, u_ref, v_ref, u0_ref, u1_ref, v_out_ref):
    rows, width = u_ref.shape[2:]
    place = lax.broadcasted_iota(jnp.int32, (width, rows), 0)
    for tile, u_out in ((0, u0_ref), (1, u1_ref)):
        keep = place < rank_ref[tile, 0]
        v_out_ref[tile] = jnp.where(keep, turned(v_ref[tile, 0]), 0.0).astype(BF16)
        u_out[...] = jnp.where(keep, turned(u_ref[tile, 0]), 0.0).astype(BF16)


def solve_kernel(count, place_ref, inverse_ref, *refs):
    held, (s0_ref, s1_ref) = refs[:count], refs[count:]
    chunk = held[0].shape[2]
    totals = [None, None]
    for shift in range(count):
        block = lax.rem(place_ref[1] - shift + count, count)
        if len(inverse_ref.shape) == 3:
            piece = inverse_ref[block]
        else:
            piece = inverse_ref[:, pl.ds(pl.multiple_of(block * chunk, chunk), chunk)]
        for tile in range(2):
            term = contract(held[shift][tile], piece, NT)
            totals[tile] = term if totals[tile] is None else totals[tile] + term
    s0_ref[...] = totals[0].astype(BF16)
    s1_ref[...] = totals[1].astype(BF16)


def eliminate(blocks):
    size = blocks[0].shape[0]
    lanes = lax.broadcasted_iota(jnp.int32, (size, size), 1)
    rows = lax.broadcasted_iota(jnp.int32, (size, 2 * size), 0)
    unit = (lanes == lax.broadcasted_iota(jnp.int32, (size, size), 0)).astype(F32)
    held = [jnp.concatenate([block, unit], axis=1) for block in blocks]
    for step in range(size):
        for index, value in enumerate(held):
            pivot = value[step : step + 1, step : step + 1]
            root = lax.rsqrt(pivot)
            row = value[step : step + 1, :] * root
            column = value[:, step : step + 1] * root
            held[index] = jnp.where(
                rows > step, value - column * row, jnp.where(rows == step, row, value)
            )
    return [value[:, size:] for value in held]


def inverse_factors(grams):
    width = grams[0].shape[0]
    unit = (
        lax.broadcasted_iota(jnp.int32, (width, width), 0)
        == lax.broadcasted_iota(jnp.int32, (width, width), 1)
    ).astype(F32)
    rests = list(grams)
    sides = [unit for _ in grams]
    found = [[] for _ in grams]
    for start in range(0, width, STEP):
        small = eliminate([rest[:STEP, :STEP] for rest in rests])
        for index in range(len(grams)):
            rest, side = rests[index], sides[index]
            left = contract(small[index], rest[:STEP, :], NN, HIGH)
            right = contract(small[index], side[:STEP, :], NN, HIGH)
            found[index].append(right)
            if start + STEP < width:
                below = left[:, STEP:]
                rests[index] = rest[STEP:, STEP:] - contract(below, below, TN, HIGH)
                sides[index] = side[STEP:, :] - contract(below, right, TN, HIGH)
    return [jnp.concatenate(rows, axis=0) for rows in found]


def tile_kernel(
    n_row, n_col, columns, place_ref, rank_ref, u_ref, v_ref, w_ref, *refs
):
    far_u, refs = refs[:n_row], refs[n_row:]
    far_s, refs = refs[:n_row], refs[n_row:]
    near_u, refs = refs[:n_col], refs[n_col:]
    near_s, refs = refs[:n_col], refs[n_col:]
    new_u_ref, new_v_ref, cu, cs, ru, rs, y_ref, sem = refs
    copies = []
    for flip in range(n_row):
        source = lax.bitwise_xor(place_ref[0], flip)
        for index, (array, room) in enumerate(((far_u[flip], cu), (far_s[flip], cs))):
            copies.append(
                pltpu.make_async_copy(
                    array,
                    room.at[lax.div(source, n_col), lax.rem(source, n_col)],
                    sem.at[index * n_row + flip],
                )
            )
    for shift in range(n_col):
        source = lax.rem(place_ref[1] - shift + n_col, n_col)
        for index, (array, room) in enumerate(((near_u[shift], ru), (near_s[shift], rs))):
            copies.append(
                pltpu.make_async_copy(
                    array, room.at[source], sem.at[2 * n_row + index * n_col + shift]
                )
            )
    for copy in copies:
        copy.start()
    height, width = u_ref.shape[3:]
    chunk = height // n_col
    spot = lax.broadcasted_iota(jnp.int32, (1, width), 1)
    eye = lax.broadcasted_iota(jnp.int32, (width, width), 0) == lax.broadcasted_iota(
        jnp.int32, (width, width), 1
    )
    keeps = [(spot < rank_ref[c, 0, 0]).astype(F32) for c in range(columns)]
    smalls = []
    for c in range(columns):
        half = keeps[c].astype(BF16)
        smalls.append(contract(v_ref[c, 0, 0] * half, w_ref[c, 0, 0] * half, TN))
    for copy in copies:
        copy.wait()
    couplings, grams, pairs = [], [], []
    for c in range(columns):
        half = keeps[c].astype(BF16)
        om = w_ref[c, 0, 0] * half
        ou = u_ref[c, 0, 0] * half
        coupling = sum(contract(rs[a], cs[c, a], NT) for a in range(n_col))
        right = sum(
            contract(cu[c, a], om[a * chunk : (a + 1) * chunk], NN) for a in range(n_col)
        )
        turn = contract(coupling, right, NN, HIGH)
        small_parts, turn_parts = parts(smalls[c]), parts(-turn)
        gram = jnp.where(eye, 1.0 - keeps[c], 0.0)
        pair = [jnp.zeros((width, width), F32), jnp.zeros((width, width), F32)]
        for a in range(n_col):
            own = ou[a * chunk : (a + 1) * chunk]
            far = ru[a]
            far_turned = turned(far).astype(BF16)
            y = sum(contract(own, part, NN) for part in small_parts)
            y = y + sum(contract(far_turned, part, NN) for part in turn_parts)
            y_ref[c, pl.ds(a * chunk, chunk), :] = y
            gram = gram + contract(y, y, TN, HIGH)
            own_turned = turned(own).astype(BF16)
            for part in parts(y):
                pair[0] = pair[0] + contract(own_turned, part, NN)
                pair[1] = pair[1] + contract(far, part, NN)
        couplings.append(coupling)
        grams.append(gram)
        pairs.append(pair)
    inverses = inverse_factors(grams)
    factor = math.sqrt(height)
    for c in range(columns):
        half = keeps[c].astype(BF16)
        ov = v_ref[c, 0, 0] * half
        scaled = inverses[c] * factor
        own = contract(pairs[c][0], inverses[c], NT, HIGH) * (1.0 / factor)
        far = contract(pairs[c][1], inverses[c], NT, HIGH) * (1.0 / factor)
        far = -contract(couplings[c], far, TN, HIGH)
        own_parts, far_parts = parts(own), parts(far)
        for a in range(n_col):
            rows = pl.ds(a * chunk, chunk)
            new_u_ref[c, 0, 0, rows, :] = contract(y_ref[c, rows, :], scaled, NT, HIGH)
            panel = turned(cu[c, a]).astype(BF16)
            value = sum(
                contract(ov[a * chunk : (a + 1) * chunk], part, NN) for part in own_parts
            )
            new_v_ref[c, 0, 0, rows, :] = value + sum(
                contract(panel, part, NN) for part in far_parts
            )


def on_device(panel_u, panel_v, panel_rank, diag_inverse, tile_u, tile_v, tile_rank, sketch):
    n_row, n_col = lax.axis_size("row"), lax.axis_size("col")
    chunk, width = panel_u.shape[2:]
    columns, height = tile_u.shape[0], tile_u.shape[3]
    place = jnp.stack([lax.axis_index("row"), lax.axis_index("col")]).astype(jnp.int32)
    half = jax.ShapeDtypeStruct((width, chunk), BF16)
    u0, u1, v_both = pl.pallas_call(
        mask_kernel,
        out_shape=(half, half, jax.ShapeDtypeStruct((2, width, chunk), BF16)),
        in_specs=[SMEM, VMEM, VMEM],
        out_specs=(VMEM, VMEM, VMEM),
        name="mask",
    )(panel_rank, panel_u, panel_v)

    def across(value):
        pairs = []
        for row in range(n_row):
            for col in range(n_col):
                pairs.append(
                    (row * n_col + col, (row // n_col * n_col + col) * n_col + row % n_col)
                )
        return lax.ppermute(value, ("row", "col"), pairs)

    def flip(value, mask):
        return lax.ppermute(value, "row", [(i, i ^ mask) for i in range(n_row)])

    def plane(value):
        same = {0: value}
        for mask in range(2, n_row, 2):
            same[mask] = flip(value, mask)
        full = dict(same)
        for mask in range(0, n_row, 2):
            full[mask + 1] = flip(same[mask], 1)
        return [full[mask] for mask in range(n_row)]

    def along(value):
        found = [value]
        for shift in range(1, n_col):
            pairs = [(i, (i + shift) % n_col) for i in range(n_col)]
            found.append(lax.ppermute(value, "col", pairs))
        return found

    held = [v_both]
    for shift in range(1, n_col):
        pairs = [(i, i + shift) for i in range(n_col - shift)]
        held.append(lax.ppermute(v_both, "col", pairs))
    inverse = diag_inverse
    if chunk % 128 != 0:
        inverse = diag_inverse.reshape(chunk, n_col, chunk).transpose(1, 0, 2)
    s0, s1 = pl.pallas_call(
        functools.partial(solve_kernel, n_col),
        out_shape=(half, half),
        in_specs=[SMEM] + [VMEM] * (1 + n_col),
        out_specs=(VMEM, VMEM),
        name="solve",
    )(place, inverse, *held)
    far_u, near_u = plane(across(u0)), along(u1)
    far_s, near_s = plane(across(s0)), along(s1)
    result = jax.ShapeDtypeStruct(tile_u.shape, F32)
    moved = far_u + far_s + near_u + near_s
    return pl.pallas_call(
        functools.partial(tile_kernel, n_row, n_col, columns),
        out_shape=(result, result),
        in_specs=[SMEM, SMEM, VMEM, VMEM, VMEM] + [ANY] * len(moved),
        out_specs=(VMEM, VMEM),
        scratch_shapes=[
            pltpu.VMEM((columns, n_col, width, chunk), BF16),
            pltpu.VMEM((columns, n_col, width, chunk), BF16),
            pltpu.VMEM((n_col, width, chunk), BF16),
            pltpu.VMEM((n_col, width, chunk), BF16),
            pltpu.VMEM((columns, height, width), F32),
            pltpu.SemaphoreType.DMA((2 * n_row + 2 * n_col,)),
        ],
        compiler_params=pltpu.CompilerParams(vmem_limit_bytes=48 * 1024 * 1024),
        name="tiles",
    )(place, tile_rank, tile_u, tile_v, sketch, *moved)


def solution(mesh):
    n_row, n_col = mesh.shape["row"], mesh.shape["col"]
    assert n_row % n_col == 0
    wide = P(None, "row", "col", None)
    tile = P(None, "row", "col", None, None)
    return jax.shard_map(
        on_device,
        mesh=mesh,
        in_specs=(wide, wide, P(None, "row"), P("col", None), tile, tile, P(None, "row", "col"), tile),
        out_specs=(tile, tile),
        check_vma=False,
    )
```

```python
import functools
import math

import jax
import jax.numpy as jnp
from jax import lax
from jax.experimental import pallas as pl
from jax.experimental.pallas import tpu as pltpu
from jax.sharding import PartitionSpec as P


F32 = jnp.float32
BF16 = jnp.bfloat16
HIGH = lax.Precision.HIGHEST
GROUP = 8
VMEM = pl.BlockSpec(memory_space=pltpu.VMEM)
SMEM = pl.BlockSpec(memory_space=pltpu.SMEM)
ANY = pl.BlockSpec(memory_space=pl.ANY)

NN = ((1,), (0,))
NT = ((1,), (1,))


def contract(a, b, dims, precision=None):
    return lax.dot_general(
        a, b, (dims, ((), ())), preferred_element_type=F32, precision=precision
    )


def stacked(value):
    head = value.astype(BF16)
    value = value - head.astype(F32)
    middle = value.astype(BF16)
    return jnp.concatenate([head, middle, (value - middle.astype(F32)).astype(BF16)], axis=0)


def folded(value):
    size = value.shape[0] // 3
    return value[:size] + (value[size : 2 * size] + value[2 * size :])


def below(width, rank, axis):
    shape = (width, 1) if axis == 0 else (1, width)
    return (lax.broadcasted_iota(jnp.int32, shape, axis) < rank).astype(F32)


def solve_kernel(count, rank_ref, inverse_ref, *refs):
    held, (s0_ref, s1_ref) = refs[:count], refs[count:]
    width, chunk = held[0].shape[2:]
    here = lax.axis_index("col")
    totals = [None, None]
    for shift in range(count):
        block = lax.rem(here - shift + count, count)
        if len(inverse_ref.shape) == 3:
            piece = inverse_ref[block]
        else:
            piece = inverse_ref[:, pl.ds(pl.multiple_of(block * chunk, chunk), chunk)]
        for tile in range(2):
            term = contract(held[shift][tile, 0], piece, NT)
            totals[tile] = term if totals[tile] is None else totals[tile] + term
    s0_ref[...] = (totals[0] * below(width, rank_ref[0, 0], 0)).astype(BF16)
    s1_ref[...] = (totals[1] * below(width, rank_ref[0, 1], 0)).astype(BF16)


def small_kernel(columns, rank_ref, v_ref, w_ref, out_ref):
    width = v_ref.shape[3]
    for c in range(columns):
        rank = rank_ref[0, 0, c]
        value = contract(w_ref[c, 0, 0], v_ref[c, 0, 0], NT)
        out_ref[c] = value * below(width, rank, 0) * below(width, rank, 1)


def eliminate(blocks):
    size = blocks[0].shape[0]
    count = size // GROUP
    unit = (
        lax.broadcasted_iota(jnp.int32, (size, size), 1)
        == lax.broadcasted_iota(jnp.int32, (size, size), 0)
    ).astype(F32)
    shape = (GROUP, 2 * size)
    sub = lax.broadcasted_iota(jnp.int32, shape, 0)
    held = []
    for block in blocks:
        both = jnp.concatenate([block, unit], axis=1)
        held.append([both[g * GROUP : (g + 1) * GROUP] for g in range(count)])

    def row_of(value, index):
        return jnp.broadcast_to(value[index : index + 1, :], shape)

    for g in range(count):
        for rows in held:
            columns = []
            for j in range(GROUP):
                spot = g * GROUP + j
                columns.append(
                    [jnp.broadcast_to(rows[h][:, spot : spot + 1], shape) for h in range(g, count)]
                )
            roots = []
            for j in range(GROUP):
                root = lax.rsqrt(row_of(columns[j][0], j))
                scaled = [value * root for value in columns[j]]
                scaled[0] = jnp.where(sub > j, scaled[0], 0.0)
                columns[j] = scaled
                roots.append(root)
                for k in range(j + 1, GROUP):
                    weight = row_of(scaled[0], k)
                    columns[k] = [a - b * weight for a, b in zip(columns[k], scaled)]
            top = rows[g]
            done = []
            for j in range(GROUP):
                row = row_of(top, j) * roots[j]
                done.append(row)
                top = jnp.where(sub == j, row, top - columns[j][0] * row)
            rows[g] = top
            for h in range(g + 1, count):
                for j in range(GROUP):
                    rows[h] = rows[h] - columns[j][h - g] * done[j]
    return [jnp.concatenate(rows, axis=0)[:, size:] for rows in held]


def block_sizes(width):
    sizes = []
    while width > 0:
        sizes.append(min(64, width))
        width -= sizes[-1]
    return sizes


def inverse_factors(grams):
    width = grams[0].shape[0]
    unit = (
        lax.broadcasted_iota(jnp.int32, (width, width), 0)
        == lax.broadcasted_iota(jnp.int32, (width, width), 1)
    ).astype(F32)
    rests = list(grams)
    sides = [unit for _ in grams]
    found = [[] for _ in grams]
    for size in block_sizes(width):
        smalls = eliminate([rest[:size, :size] for rest in rests])
        for index, small in enumerate(smalls):
            rest, side = rests[index], sides[index]
            right = contract(small, side[:size], NN, HIGH)
            found[index].append(right)
            if rest.shape[0] > size:
                down = contract(rest[size:, :size], small, NT, HIGH)
                across = contract(small, rest[:size, size:], NN, HIGH)
                rests[index] = rest[size:, size:] - contract(down, across, NN, HIGH)
                sides[index] = side[size:] - contract(down, right, NN, HIGH)
    return [jnp.concatenate(rows, axis=0) for rows in found]


def tile_kernel(n_row, n_col, columns, rank_ref, small_ref, u_ref, v_ref, w_ref, *refs):
    far_u, refs = refs[:n_row], refs[n_row:]
    far_s, refs = refs[:n_row], refs[n_row:]
    near_u, refs = refs[:n_col], refs[n_col:]
    near_s, refs = refs[:n_col], refs[n_col:]
    new_u_ref, new_v_ref, cu, cs, ru, rs, y_ref, sem = refs
    here = (lax.axis_index("row"), lax.axis_index("col"))
    copies = []
    for flip in range(n_row):
        source = lax.bitwise_xor(here[0], flip)
        for index, (array, room) in enumerate(((far_u[flip], cu), (far_s[flip], cs))):
            spot = room.at[lax.div(source, n_col), lax.rem(source, n_col)]
            copies.append(pltpu.make_async_copy(array, spot, sem.at[index * n_row + flip]))
    for shift in range(n_col):
        source = lax.rem(here[1] - shift + n_col, n_col)
        for index, (array, room) in enumerate(((near_u[shift], ru), (near_s[shift], rs))):
            copies.append(
                pltpu.make_async_copy(
                    array, room.at[source], sem.at[2 * n_row + index * n_col + shift]
                )
            )
    for copy in copies:
        copy.start()
    width, height = u_ref.shape[3:]
    chunk = height // n_col
    spans = [slice(a * chunk, (a + 1) * chunk) for a in range(n_col)]
    eye = lax.broadcasted_iota(jnp.int32, (width, width), 0) == lax.broadcasted_iota(
        jnp.int32, (width, width), 1
    )
    across = [below(width, rank_ref[0, 0, c], 1) for c in range(columns)]
    down = [below(width, rank_ref[0, 0, c], 0) for c in range(columns)]
    own_parts = [stacked(small_ref[c]) for c in range(columns)]
    for copy in copies:
        copy.wait()
    couplings, far_parts = [], []
    for c in range(columns):
        coupling = sum(contract(rs[a], cs[c, a], NT) for a in range(n_col))
        right = sum(contract(w_ref[c, 0, 0, :, spans[a]], cu[c, a], NT) for a in range(n_col))
        couplings.append(coupling)
        far_parts.append(stacked(-contract(right * down[c], coupling, NT, HIGH)))
    grams = [jnp.where(eye, 1.0 - across[c], 0.0) for c in range(columns)]
    for a in range(n_col):
        for c in range(columns):
            y = folded(
                contract(own_parts[c], u_ref[c, 0, 0, :, spans[a]], NN)
                + contract(far_parts[c], ru[a], NN)
            )
            y_ref[c, a] = y
            grams[c] = grams[c] + contract(y, y, NT, HIGH)
    inverses = inverse_factors(grams)
    own = [jnp.zeros((3 * width, width), F32) for _ in range(columns)]
    far = [jnp.zeros((3 * width, width), F32) for _ in range(columns)]
    for a in range(n_col):
        for c in range(columns):
            y = stacked(y_ref[c, a])
            own[c] = own[c] + contract(y, u_ref[c, 0, 0, :, spans[a]], NT)
            far[c] = far[c] + contract(y, ru[a], NT)
    factor = math.sqrt(height)
    for c in range(columns):
        scaled = inverses[c] * factor
        for a in range(n_col):
            new_u_ref[c, 0, 0, :, spans[a]] = contract(scaled, y_ref[c, a], NN, HIGH)
        scaled = inverses[c] * (1.0 / factor)
        left = contract(scaled, folded(own[c]) * across[c], NN, HIGH)
        right = contract(scaled, -folded(far[c]), NN, HIGH)
        left, right = stacked(left), stacked(contract(right, couplings[c], NN, HIGH))
        for a in range(n_col):
            new_v_ref[c, 0, 0, :, spans[a]] = folded(
                contract(left, v_ref[c, 0, 0, :, spans[a]], NN) + contract(right, cu[c, a], NN)
            )


def on_device(panel_u, panel_v, panel_rank, diag_inverse, tile_u, tile_v, tile_rank, sketch):
    n_row, n_col = lax.axis_size("row"), lax.axis_size("col")
    panel_u, panel_v, tile_u, tile_v, sketch = (
        jnp.swapaxes(value, -1, -2) for value in (panel_u, panel_v, tile_u, tile_v, sketch)
    )
    panel_rank, tile_rank = jnp.swapaxes(panel_rank, 0, 1), jnp.moveaxis(tile_rank, 0, -1)
    width, chunk = panel_u.shape[2:]
    columns = tile_u.shape[0]
    half = jax.ShapeDtypeStruct((width, chunk), BF16)

    def across(value):
        pairs = []
        for row in range(n_row):
            for col in range(n_col):
                pairs.append(
                    (row * n_col + col, (row // n_col * n_col + col) * n_col + row % n_col)
                )
        return lax.ppermute(value, ("row", "col"), pairs)

    def flip(value, mask):
        return lax.ppermute(value, "row", [(i, i ^ mask) for i in range(n_row)])

    def plane(value):
        same = {0: value}
        for mask in range(2, n_row, 2):
            same[mask] = flip(value, mask)
        full = dict(same)
        for mask in range(0, n_row, 2):
            full[mask + 1] = flip(same[mask], 1)
        return [full[mask] for mask in range(n_row)]

    def along(value):
        found = [value]
        for shift in range(1, n_col):
            pairs = [(i, (i + shift) % n_col) for i in range(n_col)]
            found.append(lax.ppermute(value, "col", pairs))
        return found

    held = [panel_v]
    for shift in range(1, n_col):
        pairs = [(i, i + shift) for i in range(n_col - shift)]
        held.append(lax.ppermute(panel_v, "col", pairs))
    inverse = diag_inverse
    if chunk % 128 != 0:
        inverse = diag_inverse.reshape(chunk, n_col, chunk).transpose(1, 0, 2)
    s0, s1 = pl.pallas_call(
        functools.partial(solve_kernel, n_col),
        out_shape=(half, half),
        in_specs=[SMEM] + [VMEM] * (1 + n_col),
        out_specs=(VMEM, VMEM),
        name="solve",
    )(panel_rank, inverse, *held)
    small = pl.pallas_call(
        functools.partial(small_kernel, columns),
        out_shape=jax.ShapeDtypeStruct((columns, width, width), F32),
        in_specs=[SMEM, VMEM, VMEM],
        out_specs=VMEM,
        name="small",
    )(tile_rank, tile_v, sketch)
    far_u, near_u = plane(across(panel_u[0, 0])), along(panel_u[1, 0])
    far_s, near_s = plane(across(s0)), along(s1)
    result = jax.ShapeDtypeStruct(tile_u.shape, F32)
    moved = far_u + far_s + near_u + near_s
    room = pltpu.VMEM((columns, n_col, width, chunk), BF16)
    near_room = pltpu.VMEM((n_col, width, chunk), BF16)
    new_u, new_v = pl.pallas_call(
        functools.partial(tile_kernel, n_row, n_col, columns),
        out_shape=(result, result),
        in_specs=[SMEM] + [VMEM] * 4 + [ANY] * len(moved),
        out_specs=(VMEM, VMEM),
        scratch_shapes=[
            room,
            room,
            near_room,
            near_room,
            pltpu.VMEM((columns, n_col, width, chunk), F32),
            pltpu.SemaphoreType.DMA((2 * n_row + 2 * n_col,)),
        ],
        compiler_params=pltpu.CompilerParams(vmem_limit_bytes=40 * 1024 * 1024),
        name="tiles",
    )(tile_rank, small, tile_u, tile_v, sketch, *moved)
    return jnp.swapaxes(new_u, -1, -2), jnp.swapaxes(new_v, -1, -2)


def solution(mesh):
    n_row, n_col = mesh.shape["row"], mesh.shape["col"]
    assert n_row % n_col == 0
    wide = P(None, "row", "col", None)
    tile = P(None, "row", "col", None, None)
    return jax.shard_map(
        on_device,
        mesh=mesh,
        in_specs=(wide, wide, P(None, "row"), P("col", None), tile, tile, P(None, "row", "col"), tile),
        out_specs=(tile, tile),
        check_vma=False,
    )
```

```python
import functools
import math

import jax
import jax.numpy as jnp
from jax import lax
from jax.experimental import pallas as pl
from jax.experimental.pallas import tpu as pltpu
from jax.sharding import PartitionSpec as P


F32 = jnp.float32
BF16 = jnp.bfloat16
HIGH = lax.Precision.HIGHEST
GROUP = 8
SHARE_ROWS = 32
VMEM = pl.BlockSpec(memory_space=pltpu.VMEM)
SMEM = pl.BlockSpec(memory_space=pltpu.SMEM)
HBM = pl.BlockSpec(memory_space=pltpu.HBM)

NN = ((1,), (0,))
NT = ((1,), (1,))


def contract(a, b, dims, precision=None):
    return lax.dot_general(
        a, b, (dims, ((), ())), preferred_element_type=F32, precision=precision
    )


def stacked(value):
    head = value.astype(BF16)
    value = value - head.astype(F32)
    middle = value.astype(BF16)
    return jnp.concatenate([head, middle, (value - middle.astype(F32)).astype(BF16)], axis=0)


def folded(value):
    size = value.shape[0] // 3
    return value[:size] + (value[size : 2 * size] + value[2 * size :])


def below(width, rank, axis):
    shape = (width, 1) if axis == 0 else (1, width)
    return (lax.broadcasted_iota(jnp.int32, shape, axis) < rank).astype(F32)


def pack_kernel(shares, rank_ref, u_ref, v_ref, inverse_ref, *outs):
    width = u_ref.shape[2]
    for tile in range(2):
        out_ref = outs[tile]
        keep = below(width, rank_ref[0, tile], 0)
        out_ref[0] = u_ref[tile, 0]
        out_ref[1] = (v_ref[tile, 0].astype(F32) * keep).astype(BF16)
    rows = outs[2].shape[0]
    start = lax.rem(lax.axis_index("row"), shares) * rows
    outs[2][...] = inverse_ref[pl.ds(pl.multiple_of(start, rows), rows), :]


def join_kernel(*refs):
    for index, ref in enumerate(refs[:-1]):
        refs[-1][index] = ref[...]


def small_kernel(columns, rank_ref, v_ref, w_ref, out_ref):
    width = v_ref.shape[3]
    for c in range(columns):
        rank = rank_ref[0, 0, c]
        value = contract(w_ref[c, 0, 0], v_ref[c, 0, 0], NT)
        out_ref[c] = value * below(width, rank, 0) * below(width, rank, 1)


def eliminate(blocks):
    size = blocks[0].shape[0]
    count = size // GROUP
    unit = (
        lax.broadcasted_iota(jnp.int32, (size, size), 1)
        == lax.broadcasted_iota(jnp.int32, (size, size), 0)
    ).astype(F32)
    shape = (GROUP, 2 * size)
    sub = lax.broadcasted_iota(jnp.int32, shape, 0)
    held = []
    for block in blocks:
        both = jnp.concatenate([block, unit], axis=1)
        held.append([both[g * GROUP : (g + 1) * GROUP] for g in range(count)])

    def row_of(value, index):
        return jnp.broadcast_to(value[index : index + 1, :], shape)

    for g in range(count):
        for rows in held:
            columns = []
            for j in range(GROUP):
                spot = g * GROUP + j
                columns.append(
                    [jnp.broadcast_to(rows[h][:, spot : spot + 1], shape) for h in range(g, count)]
                )
            roots = []
            for j in range(GROUP):
                root = lax.rsqrt(row_of(columns[j][0], j))
                scaled = [value * root for value in columns[j]]
                scaled[0] = jnp.where(sub > j, scaled[0], 0.0)
                columns[j] = scaled
                roots.append(root)
                for k in range(j + 1, GROUP):
                    weight = row_of(scaled[0], k)
                    columns[k] = [a - b * weight for a, b in zip(columns[k], scaled)]
            top = rows[g]
            done = []
            for j in range(GROUP):
                row = row_of(top, j) * roots[j]
                done.append(row)
                top = jnp.where(sub == j, row, top - columns[j][0] * row)
            rows[g] = top
            for h in range(g + 1, count):
                for j in range(GROUP):
                    rows[h] = rows[h] - columns[j][h - g] * done[j]
    return [jnp.concatenate(rows, axis=0)[:, size:] for rows in held]


def block_sizes(width):
    sizes = []
    while width > 0:
        sizes.append(min(64, width))
        width -= sizes[-1]
    return sizes


def inverse_factors(grams):
    width = grams[0].shape[0]
    unit = (
        lax.broadcasted_iota(jnp.int32, (width, width), 0)
        == lax.broadcasted_iota(jnp.int32, (width, width), 1)
    ).astype(F32)
    rests = list(grams)
    sides = [unit for _ in grams]
    found = [[] for _ in grams]
    for size in block_sizes(width):
        smalls = eliminate([rest[:size, :size] for rest in rests])
        for index, small in enumerate(smalls):
            rest, side = rests[index], sides[index]
            right = contract(small, side[:size], NN, HIGH)
            found[index].append(right)
            if rest.shape[0] > size:
                down = contract(rest[size:, :size], small, NT, HIGH)
                across = contract(small, rest[:size, size:], NN, HIGH)
                rests[index] = rest[size:, size:] - contract(down, across, NN, HIGH)
                sides[index] = side[size:] - contract(down, right, NN, HIGH)
    return [jnp.concatenate(rows, axis=0) for rows in found]


def spread_place(value, n_col):
    return value % 2 * (n_col // 2) + value // 2


def gather_place(value, n_col):
    return lax.rem(value, n_col // 2) * 2 + lax.div(value, n_col // 2)


def tile_kernel(n_row, n_col, columns, shares, rank_ref, small_ref, u_ref, v_ref, w_ref, inverse_ref, *refs):
    far, near, refs = refs[:n_row], refs[n_row : n_row + n_col], refs[n_row + n_col :]
    pieces, refs = refs[:shares], refs[shares:]
    new_u_ref, new_v_ref, cu, cv, ru, rv, full, y_ref, sem, share_sem, own_sem = refs
    here = (lax.axis_index("row"), lax.axis_index("col"))
    rows = full.shape[2]
    copies = []
    for flip in range(shares):
        spot = lax.rem(lax.bitwise_xor(here[0], flip), shares)
        for shift in range(1, n_col):
            plane = lax.rem(here[1] - shift + n_col, n_col)
            copies.append(
                pltpu.make_async_copy(
                    pieces[flip].at[shift - 1], full.at[plane, spot], share_sem.at[flip, shift - 1]
                )
            )
    for share in range(shares):
        copies.append(
            pltpu.make_async_copy(
                inverse_ref.at[pl.ds(share * rows, rows)], full.at[here[1], share], own_sem.at[share]
            )
        )
    for flip in range(n_row):
        source = lax.bitwise_xor(here[0], flip)
        chunk_of = lax.bitwise_xor(gather_place(lax.rem(source, n_col), n_col), here[1])
        spot = (lax.div(source, n_col), chunk_of)
        for index, room in enumerate((cu, cv)):
            copies.append(
                pltpu.make_async_copy(
                    far[flip].at[index], room.at[spot], sem.at[index, flip]
                )
            )
    for shift in range(n_col):
        source = lax.rem(here[1] - shift + n_col, n_col)
        for index, room in enumerate((ru, rv)):
            copies.append(
                pltpu.make_async_copy(
                    near[shift].at[index], room.at[source], sem.at[index, n_row + shift]
                )
            )
    for copy in copies:
        copy.start()
    width, height = u_ref.shape[3:]
    chunk = height // n_col
    spans = [slice(a * chunk, (a + 1) * chunk) for a in range(n_col)]
    eye = lax.broadcasted_iota(jnp.int32, (width, width), 0) == lax.broadcasted_iota(
        jnp.int32, (width, width), 1
    )
    across = [below(width, rank_ref[0, 0, c], 1) for c in range(columns)]
    own_parts = [stacked(small_ref[c]) for c in range(columns)]
    for copy in copies:
        copy.wait()
    couplings, far_parts = [], []
    panels = jnp.concatenate(
        [
            jnp.concatenate([cv[c, a] for c in range(columns)] + [rv[a]], axis=0)
            for a in range(n_col)
        ],
        axis=1,
    )
    solved = []
    for a in range(n_col):
        end = (a + 1) * chunk
        piece = full[a].reshape(chunk, height)[:, :end]
        solved.append(contract(panels[:, :end], piece, NT).astype(BF16))
    for c in range(columns):
        coupling = sum(
            contract(value[columns * width :], value[c * width : (c + 1) * width], NT)
            for value in solved
        )
        right = sum(contract(w_ref[c, 0, 0, :, spans[a]], cu[c, a], NT) for a in range(n_col))
        couplings.append(coupling)
        right = right * below(width, rank_ref[0, 0, c], 0)
        far_parts.append(stacked(-contract(right, coupling, NT, HIGH)))
    grams = [jnp.where(eye, 1.0 - across[c], 0.0) for c in range(columns)]
    for a in range(n_col):
        for c in range(columns):
            y = folded(
                contract(own_parts[c], u_ref[c, 0, 0, :, spans[a]], NN)
                + contract(far_parts[c], ru[a], NN)
            )
            y_ref[c, a] = y
            grams[c] = grams[c] + contract(y, y, NT, HIGH)
    inverses = inverse_factors(grams)
    own = [jnp.zeros((3 * width, width), F32) for _ in range(columns)]
    far = [jnp.zeros((3 * width, width), F32) for _ in range(columns)]
    for a in range(n_col):
        for c in range(columns):
            y = stacked(y_ref[c, a])
            own[c] = own[c] + contract(y, u_ref[c, 0, 0, :, spans[a]], NT)
            far[c] = far[c] + contract(y, ru[a], NT)
    factor = math.sqrt(height)
    for c in range(columns):
        scaled = inverses[c] * factor
        for a in range(n_col):
            new_u_ref[c, 0, 0, :, spans[a]] = contract(scaled, y_ref[c, a], NN, HIGH)
        scaled = inverses[c] * (1.0 / factor)
        left = contract(scaled, folded(own[c]) * across[c], NN, HIGH)
        right = contract(scaled, -folded(far[c]), NN, HIGH)
        left, right = stacked(left), stacked(contract(right, couplings[c], NN, HIGH))
        for a in range(n_col):
            new_v_ref[c, 0, 0, :, spans[a]] = folded(
                contract(left, v_ref[c, 0, 0, :, spans[a]], NN) + contract(right, cu[c, a], NN)
            )


def share_count(n_row, chunk):
    return max(1, min(n_row, chunk // SHARE_ROWS))


def whole(panel_u, panel_v, panel_rank, diag_inverse, tile_u, tile_v, tile_rank, sketch):
    n_row, n_col = lax.axis_size("row"), lax.axis_size("col")
    panel_u, panel_v, tile_u, tile_v, sketch = (
        jnp.swapaxes(value, -1, -2) for value in (panel_u, panel_v, tile_u, tile_v, sketch)
    )
    panel_rank, tile_rank = jnp.swapaxes(panel_rank, 0, 1), jnp.moveaxis(tile_rank, 0, -1)
    width, chunk = panel_u.shape[2:]
    columns = tile_u.shape[0]
    pair = jax.ShapeDtypeStruct((2, width, chunk), BF16)

    def across(value):
        pairs = []
        for row in range(n_row):
            for col in range(n_col):
                spot = spread_place(row % n_col ^ col, n_col)
                pairs.append((row * n_col + col, (row // n_col * n_col + spot) * n_col + row % n_col))
        return lax.ppermute(value, ("row", "col"), pairs)

    def flip(value, mask):
        return lax.ppermute(value, "row", [(i, i ^ mask) for i in range(n_row)])

    def plane(value, count):
        same = {0: value}
        for mask in range(2, count, 2):
            same[mask] = flip(value, mask)
        full = dict(same)
        for mask in range(0, count, 2):
            full[mask + 1] = flip(same[mask], 1)
        return [full[mask] for mask in range(count)]

    def along(value):
        found = [value]
        for shift in range(1, n_col):
            pairs = [(i, (i + shift) % n_col) for i in range(n_col)]
            found.append(lax.ppermute(value, "col", pairs))
        return found

    shares = share_count(n_row, chunk)
    part = jax.ShapeDtypeStruct((chunk // shares, diag_inverse.shape[1]), BF16)
    far, near, share = pl.pallas_call(
        functools.partial(pack_kernel, shares),
        out_shape=(pair, pair, part),
        in_specs=[SMEM] + [VMEM] * 3,
        out_specs=(VMEM,) * 3,
        name="pack",
    )(panel_rank, panel_u, panel_v, diag_inverse)
    far, shared = across(far), along(share)[1:]
    near, far = along(near), plane(far, n_row)
    joined = pl.pallas_call(
        join_kernel,
        out_shape=jax.ShapeDtypeStruct((n_col - 1,) + share.shape, BF16),
        in_specs=[VMEM] * (n_col - 1),
        out_specs=VMEM,
        name="join",
    )(*shared)
    pieces = plane(joined, shares)
    small = pl.pallas_call(
        functools.partial(small_kernel, columns),
        out_shape=jax.ShapeDtypeStruct((columns, width, width), F32),
        in_specs=[SMEM, VMEM, VMEM],
        out_specs=VMEM,
        name="small",
    )(tile_rank, tile_v, sketch)
    room = pltpu.VMEM((columns, n_col, width, chunk), BF16)
    near_room = pltpu.VMEM((n_col, width, chunk), BF16)
    result = jax.ShapeDtypeStruct(tile_u.shape, F32)
    new_u, new_v = pl.pallas_call(
        functools.partial(tile_kernel, n_row, n_col, columns, shares),
        out_shape=(result, result),
        in_specs=[SMEM] + [VMEM] * 4 + [HBM] * (1 + n_row + n_col + shares),
        out_specs=(VMEM, VMEM),
        scratch_shapes=[
            room,
            room,
            near_room,
            near_room,
            pltpu.VMEM((n_col, shares) + share.shape, BF16),
            pltpu.VMEM((columns, n_col, width, chunk), F32),
            pltpu.SemaphoreType.DMA((2, n_row + n_col)),
            pltpu.SemaphoreType.DMA((shares, n_col - 1)),
            pltpu.SemaphoreType.DMA((shares,)),
        ],
        compiler_params=pltpu.CompilerParams(vmem_limit_bytes=60 * 1024 * 1024),
        name="tiles",
    )(tile_rank, small, tile_u, tile_v, sketch, diag_inverse, *far, *near, *pieces)
    return jnp.swapaxes(new_u, -1, -2), jnp.swapaxes(new_v, -1, -2)


def solution(mesh):
    n_row, n_col = mesh.shape["row"], mesh.shape["col"]
    assert n_row % n_col == 0
    wide = P(None, "row", "col", None)
    tile = P(None, "row", "col", None, None)
    return jax.shard_map(
        whole,
        mesh=mesh,
        in_specs=(wide, wide, P(None, "row"), P("col", None), tile, tile, P(None, "row", "col"), tile),
        out_specs=(tile, tile),
        check_vma=False,
    )
```

```python
import functools
import math

import jax
import jax.numpy as jnp
from jax import lax
from jax.experimental import pallas as pl
from jax.experimental.pallas import tpu as pltpu
from jax.sharding import PartitionSpec as P


F32 = jnp.float32
BF16 = jnp.bfloat16
HIGH = lax.Precision.HIGHEST
GROUP = 8
SHARE_ROWS = 32
OUT_LANES = 256
VMEM = pl.BlockSpec(memory_space=pltpu.VMEM)
SMEM = pl.BlockSpec(memory_space=pltpu.SMEM)
HBM = pl.BlockSpec(memory_space=pltpu.HBM)
MIB = 1024 * 1024
LIGHT = pltpu.CompilerParams(vmem_limit_bytes=6 * MIB)

NN = ((1,), (0,))
NT = ((1,), (1,))


def contract(a, b, dims, precision=None):
    return lax.dot_general(
        a, b, (dims, ((), ())), preferred_element_type=F32, precision=precision
    )


def stacked(value, count):
    found = []
    for _ in range(count - 1):
        found.append(value.astype(BF16))
        value = value - found[-1].astype(F32)
    return jnp.concatenate(found + [value.astype(BF16)], axis=0)


def folded(value, count):
    size = value.shape[0] // count
    total = value[(count - 1) * size :]
    for index in range(count - 2, -1, -1):
        total = value[index * size : (index + 1) * size] + total
    return total


def below(width, rank, axis):
    shape = (width, 1) if axis == 0 else (1, width)
    return (lax.broadcasted_iota(jnp.int32, shape, axis) < rank).astype(F32)


def pack_kernel(shares, rank_ref, u_hbm, v_hbm, inverse_hbm, far_ref, near_ref, share_ref, v_ref, sem):
    rows, width = share_ref.shape[0], v_ref.shape[1]
    start = lax.rem(lax.axis_index("row"), shares) * rows
    part = inverse_hbm.at[pl.ds(pl.multiple_of(start, rows), rows), :]
    copies = [
        pltpu.make_async_copy(v_hbm.at[:, 0], v_ref, sem.at[0]),
        pltpu.make_async_copy(part, share_ref, sem.at[1]),
        pltpu.make_async_copy(u_hbm.at[0, 0], far_ref.at[0], sem.at[2]),
        pltpu.make_async_copy(u_hbm.at[1, 0], near_ref.at[0], sem.at[3]),
    ]
    for copy in copies:
        copy.start()
    copies[0].wait()
    for tile, out_ref in enumerate((far_ref, near_ref)):
        keep = below(width, rank_ref[0, tile], 0)
        out_ref[1] = (v_ref[tile].astype(F32) * keep).astype(BF16)
    for copy in copies[1:]:
        copy.wait()


def join_kernel(*refs):
    for index, ref in enumerate(refs[:-1]):
        refs[-1][index] = ref[...]


def eliminate(blocks):
    size = blocks[0].shape[0]
    count = size // GROUP
    unit = (
        lax.broadcasted_iota(jnp.int32, (size, size), 1)
        == lax.broadcasted_iota(jnp.int32, (size, size), 0)
    ).astype(F32)
    shape = (GROUP, 2 * size)
    sub = lax.broadcasted_iota(jnp.int32, shape, 0)
    held = []
    for block in blocks:
        both = jnp.concatenate([block, unit], axis=1)
        held.append([both[g * GROUP : (g + 1) * GROUP] for g in range(count)])

    def row_of(value, index):
        return jnp.broadcast_to(value[index : index + 1, :], shape)

    for g in range(count):
        for rows in held:
            columns = []
            for j in range(GROUP):
                spot = g * GROUP + j
                columns.append(
                    [jnp.broadcast_to(rows[h][:, spot : spot + 1], shape) for h in range(g, count)]
                )
            roots = []
            for j in range(GROUP):
                root = lax.rsqrt(row_of(columns[j][0], j))
                scaled = [value * root for value in columns[j]]
                scaled[0] = jnp.where(sub > j, scaled[0], 0.0)
                columns[j] = scaled
                roots.append(root)
                for k in range(j + 1, GROUP):
                    weight = row_of(scaled[0], k)
                    columns[k] = [a - b * weight for a, b in zip(columns[k], scaled)]
            top = rows[g]
            done = []
            for j in range(GROUP):
                row = row_of(top, j) * roots[j]
                done.append(row)
                top = jnp.where(sub == j, row, top - columns[j][0] * row)
            rows[g] = top
            for h in range(g + 1, count):
                for j in range(GROUP):
                    rows[h] = rows[h] - columns[j][h - g] * done[j]
    return [jnp.concatenate(rows, axis=0)[:, size:] for rows in held]


def block_sizes(width):
    sizes = []
    while width > 0:
        sizes.append(min(64, width))
        width -= sizes[-1]
    return sizes


def inverse_factors(grams, fillers):
    width = grams[0].shape[0]
    unit = (
        lax.broadcasted_iota(jnp.int32, (width, width), 0)
        == lax.broadcasted_iota(jnp.int32, (width, width), 1)
    ).astype(F32)
    rests = list(grams)
    sides = [unit for _ in grams]
    found = [[] for _ in grams]
    for turn, size in enumerate(block_sizes(width)):
        if turn < len(fillers):
            fillers[turn]()
        smalls = eliminate([rest[:size, :size] for rest in rests])
        for index, small in enumerate(smalls):
            rest, side = rests[index], sides[index]
            right = contract(small, side[:size], NN, HIGH)
            found[index].append(right)
            if rest.shape[0] > size:
                down = contract(rest[size:, :size], small, NT, HIGH)
                across = contract(small, rest[:size, size:], NN, HIGH)
                rests[index] = rest[size:, size:] - contract(down, across, NN, HIGH)
                sides[index] = side[size:] - contract(down, right, NN, HIGH)
    return [jnp.concatenate(rows, axis=0) for rows in found]


def six(left, right, dims):
    size, other = left.shape[0] // 3, right.shape[0] // 3
    first = contract(left, right[:other], dims)
    second = contract(left[: 2 * size], right[other : 2 * other], dims)
    third = contract(left[:size], right[2 * other :], dims)
    small = (first[2 * size :] + second[size:]) + third
    return first[:size] + ((first[size : 2 * size] + second[:size]) + small)


def three(left, right, dims):
    size, other = left.shape[0] // 2, right.shape[0] // 3
    first = contract(left, right[:other], dims)
    return first[:size] + (first[size:] + contract(left[:size], right[other : 2 * other], dims))


def spread_place(value, n_col):
    return value % 2 * (n_col // 2) + value // 2


def gather_place(value, n_col):
    return lax.rem(value, n_col // 2) * 2 + lax.div(value, n_col // 2)


def tile_kernel(n_row, n_col, columns, shares, rank_ref, *refs):
    (u_ref, v_hbm, w_hbm, inverse_ref), refs = refs[:4], refs[4:]
    far, near, refs = refs[:n_row], refs[n_row : n_row + n_col], refs[n_row + n_col :]
    pieces, refs = refs[:shares], refs[shares:]
    new_u_hbm, new_v_hbm, far_ref, near_ref, full, parts_ref, *refs = refs
    new_u_ref, new_v_ref, v_ref, w_ref, out_sem, in_sem = refs
    here = (lax.axis_index("row"), lax.axis_index("col"))

    def begin(copies):
        for copy in copies:
            copy.start()
        return copies

    def end(copies):
        for copy in copies:
            copy.wait()

    loads = begin(
        [
            pltpu.make_async_copy(v_hbm, v_ref, in_sem.at[0]),
            pltpu.make_async_copy(w_hbm, w_ref, in_sem.at[1]),
        ]
    )
    full[:, 0] = inverse_ref[...]
    for flip in range(shares):
        spot = lax.rem(lax.bitwise_xor(here[0], flip), shares)
        full[spot, 1:] = pieces[flip][...]
    for flip in range(n_row):
        source = lax.bitwise_xor(here[0], flip)
        chunk_of = lax.bitwise_xor(gather_place(lax.rem(source, n_col), n_col), here[1])
        far_ref[lax.div(source, n_col), chunk_of] = far[flip][...]
    for shift in range(n_col):
        near_ref[lax.bitwise_xor(here[1], shift)] = near[shift][...]
    width, height = u_ref.shape[3:]
    chunk = height // n_col
    spans = [slice(a * chunk, (a + 1) * chunk) for a in range(n_col)]
    eye = lax.broadcasted_iota(jnp.int32, (width, width), 0) == lax.broadcasted_iota(
        jnp.int32, (width, width), 1
    )
    across = [below(width, rank_ref[0, 0, c], 1) for c in range(columns)]

    def joined(index, c=None):
        if c is None:
            return jnp.concatenate([near_ref[a, index] for a in range(n_col)], axis=1)
        return jnp.concatenate([far_ref[c, a, index] for a in range(n_col)], axis=1)

    right = jnp.concatenate([joined(1, c) for c in range(columns)] + [joined(1)], axis=0)
    solved = []
    for a in range(n_col):
        last = (a + 1) * chunk
        shift = lax.bitwise_xor(here[1], a)
        piece = jnp.concatenate([full[share, shift] for share in range(shares)], axis=0)
        solved.append(contract(right[:, :last], piece[:, :last], NT).astype(BF16))
    solved = jnp.concatenate(solved, axis=1)
    couplings = [
        contract(solved[columns * width :], solved[c * width : (c + 1) * width], NT)
        for c in range(columns)
    ]
    end(loads)
    far_u = [joined(0, c) for c in range(columns)]
    near_u = joined(0)
    far_parts = []
    for c in range(columns):
        right = contract(w_ref[c, 0, 0], far_u[c], NT) * below(width, rank_ref[0, 0, c], 0)
        far_parts.append(stacked(-contract(right, couplings[c], NT, HIGH), 2))
    own_parts = []
    for c in range(columns):
        rank = rank_ref[0, 0, c]
        value = contract(w_ref[c, 0, 0], v_ref[c, 0, 0], NT)
        own_parts.append(stacked(value * below(width, rank, 0) * across[c], 2))
    for c in range(columns):
        for a in range(n_col):
            y = folded(
                contract(own_parts[c], u_ref[c, 0, 0, :, spans[a]], NN)
                + contract(far_parts[c], near_ref[a, 0], NN),
                2,
            )
            parts_ref[c, a] = stacked(y, 3)
    grams = []
    for c in range(columns):
        y = jnp.concatenate([parts_ref[c, a] for a in range(n_col)], axis=1)
        grams.append(six(y, y, NT) + jnp.where(eye, 1.0 - across[c], 0.0))
    own, far = [None] * columns, [None] * columns

    def project(c):
        y = jnp.concatenate([parts_ref[c, a] for a in range(n_col)], axis=1)
        own[c] = folded(contract(y, u_ref[c, 0, 0], NT), 3) * across[c]
        far[c] = folded(contract(y, near_u, NT), 3)

    inverses = inverse_factors(grams, [functools.partial(project, c) for c in range(columns)])
    factor = math.sqrt(height)
    sides = []
    for c in range(columns):
        scaled = inverses[c] * (1.0 / factor)
        left = contract(scaled, own[c], NN, HIGH)
        right = contract(contract(scaled, -far[c], NN, HIGH), couplings[c], NN, HIGH)
        sides.append((stacked(left, 2), stacked(right, 2)))
    outs = []
    reach = max(1, OUT_LANES // chunk)

    def send(index, c, a, room, target):
        if (a + 1) % reach == 0:
            lanes = slice((a + 1 - reach) * chunk, (a + 1) * chunk)
            spot = (c, 0, 0, slice(None), lanes)
            copy = pltpu.make_async_copy(room.at[spot], target.at[spot], out_sem.at[index, c, a])
            outs.extend(begin([copy]))

    for c in range(columns):
        scaled = stacked(inverses[c] * factor, 2)
        for a in range(n_col):
            new_u_ref[c, 0, 0, :, spans[a]] = three(scaled, parts_ref[c, a], NN)
            send(0, c, a, new_u_ref, new_u_hbm)
    for c in range(columns):
        left, right = sides[c]
        for a in range(n_col):
            new_v_ref[c, 0, 0, :, spans[a]] = folded(
                contract(left, v_ref[c, 0, 0, :, spans[a]], NN)
                + contract(right, far_ref[c, a, 0], NN),
                2,
            )
            send(1, c, a, new_v_ref, new_v_hbm)
    end(outs)


def in_hbm(value):
    return pltpu.with_memory_space_constraint(value, pltpu.HBM)


def share_count(n_row, chunk):
    return max(1, min(n_row, chunk // SHARE_ROWS))


def whole(panel_u, panel_v, panel_rank, diag_inverse, tile_u, tile_v, tile_rank, sketch):
    n_row, n_col = lax.axis_size("row"), lax.axis_size("col")
    panel_u, panel_v, tile_u, tile_v, sketch = (
        jnp.swapaxes(value, -1, -2) for value in (panel_u, panel_v, tile_u, tile_v, sketch)
    )
    panel_rank, tile_rank = jnp.swapaxes(panel_rank, 0, 1), jnp.moveaxis(tile_rank, 0, -1)
    width, chunk = panel_u.shape[2:]
    columns = tile_u.shape[0]
    pair = jax.ShapeDtypeStruct((2, width, chunk), BF16)

    def across(value):
        pairs = []
        for row in range(n_row):
            for col in range(n_col):
                spot = spread_place(row % n_col ^ col, n_col)
                pairs.append((row * n_col + col, (row // n_col * n_col + spot) * n_col + row % n_col))
        return lax.ppermute(value, ("row", "col"), pairs)

    def flip(value, mask):
        return lax.ppermute(value, "row", [(i, i ^ mask) for i in range(n_row)])

    def plane(value, count):
        same = {0: value}
        for mask in range(2, count, 2):
            same[mask] = flip(value, mask)
        full = dict(same)
        for mask in range(0, count, 2):
            full[mask + 1] = flip(same[mask], 1)
        return [full[mask] for mask in range(count)]

    def along(value):
        found = [value]
        for shift in range(1, n_col):
            pairs = [(i, i ^ shift) for i in range(n_col)]
            found.append(lax.ppermute(value, "col", pairs))
        return found

    shares = share_count(n_row, chunk)
    part = jax.ShapeDtypeStruct((chunk // shares, diag_inverse.shape[1]), BF16)
    far, near, share = pl.pallas_call(
        functools.partial(pack_kernel, shares),
        out_shape=(pair, pair, part),
        in_specs=[SMEM] + [HBM] * 3,
        out_specs=(VMEM,) * 3,
        scratch_shapes=[
            pltpu.VMEM((2, width, chunk), BF16),
            pltpu.SemaphoreType.DMA((4,)),
        ],
        compiler_params=LIGHT,
        name="pack",
    )(*(in_hbm(value) for value in (panel_rank, panel_u, panel_v, diag_inverse)))
    far, shared = across(far), along(share)[1:]
    near, far = along(near), plane(far, n_row)
    joined = pl.pallas_call(
        join_kernel,
        out_shape=jax.ShapeDtypeStruct((n_col - 1,) + share.shape, BF16),
        in_specs=[VMEM] * (n_col - 1),
        out_specs=VMEM,
        compiler_params=LIGHT,
        name="join",
    )(*shared)
    pieces = plane(joined, shares)
    result = jax.ShapeDtypeStruct(tile_u.shape, F32)
    new_u, new_v = pl.pallas_call(
        functools.partial(tile_kernel, n_row, n_col, columns, shares),
        out_shape=(result, result),
        in_specs=[SMEM, VMEM, HBM, HBM] + [VMEM] * (1 + n_row + n_col + shares),
        out_specs=(HBM, HBM),
        scratch_shapes=[
            pltpu.VMEM((columns, n_col, 2, width, chunk), BF16),
            pltpu.VMEM((n_col, 2, width, chunk), BF16),
            pltpu.VMEM((shares, n_col) + share.shape, BF16),
            pltpu.VMEM((columns, n_col, 3 * width, chunk), BF16),
            *[pltpu.VMEM(tile_u.shape, F32)] * 2,
            *[pltpu.VMEM(tile_u.shape, BF16)] * 2,
            pltpu.SemaphoreType.DMA((2, columns, n_col)),
            pltpu.SemaphoreType.DMA((2,)),
        ],
        compiler_params=pltpu.CompilerParams(vmem_limit_bytes=22 * MIB),
        name="tiles",
    )(in_hbm(tile_rank), tile_u, in_hbm(tile_v), in_hbm(sketch), diag_inverse.reshape((shares,) + share.shape), *far, *near, *pieces)
    return jnp.swapaxes(new_u, -1, -2), jnp.swapaxes(new_v, -1, -2)


def solution(mesh):
    n_row, n_col = mesh.shape["row"], mesh.shape["col"]
    assert n_row % n_col == 0
    wide = P(None, "row", "col", None)
    tile = P(None, "row", "col", None, None)
    return jax.shard_map(
        whole,
        mesh=mesh,
        in_specs=(wide, wide, P(None, "row"), P("col", None), tile, tile, P(None, "row", "col"), tile),
        out_specs=(tile, tile),
        check_vma=False,
    )
```

```python
import functools
import math

import jax
import jax.numpy as jnp
from jax import lax
from jax.experimental import pallas as pl
from jax.experimental.pallas import tpu as pltpu
from jax.sharding import PartitionSpec as P


F32 = jnp.float32
BF16 = jnp.bfloat16
HIGH = lax.Precision.HIGHEST
GROUP = 8
SHARE_ROWS = 32
OUT_LANES = 256
VMEM = pl.BlockSpec(memory_space=pltpu.VMEM)
SMEM = pl.BlockSpec(memory_space=pltpu.SMEM)
HBM = pl.BlockSpec(memory_space=pltpu.HBM)
MIB = 1024 * 1024
LIGHT = pltpu.CompilerParams(vmem_limit_bytes=6 * MIB)

NN = ((1,), (0,))
NT = ((1,), (1,))


def contract(a, b, dims, precision=None):
    return lax.dot_general(
        a, b, (dims, ((), ())), preferred_element_type=F32, precision=precision
    )


def stacked(value, count):
    found = []
    for _ in range(count - 1):
        found.append(value.astype(BF16))
        value = value - found[-1].astype(F32)
    return jnp.concatenate(found + [value.astype(BF16)], axis=0)


def folded(value, count):
    size = value.shape[0] // count
    total = value[(count - 1) * size :]
    for index in range(count - 2, -1, -1):
        total = value[index * size : (index + 1) * size] + total
    return total


def below(width, rank, axis):
    shape = (width, 1) if axis == 0 else (1, width)
    return (lax.broadcasted_iota(jnp.int32, shape, axis) < rank).astype(F32)


def pack_kernel(shares, rank_ref, u_hbm, v_hbm, inverse_hbm, far_ref, near_ref, share_ref, v_ref, sem):
    rows, width = share_ref.shape[0], v_ref.shape[1]
    start = lax.rem(lax.axis_index("row"), shares) * rows
    part = inverse_hbm.at[pl.ds(pl.multiple_of(start, rows), rows), :]
    copies = [
        pltpu.make_async_copy(v_hbm.at[:, 0], v_ref, sem.at[0]),
        pltpu.make_async_copy(part, share_ref, sem.at[1]),
        pltpu.make_async_copy(u_hbm.at[0, 0], far_ref.at[0], sem.at[2]),
        pltpu.make_async_copy(u_hbm.at[1, 0], near_ref.at[0], sem.at[3]),
    ]
    for copy in copies:
        copy.start()
    copies[0].wait()
    for tile, out_ref in enumerate((far_ref, near_ref)):
        keep = below(width, rank_ref[0, tile], 0)
        out_ref[1] = (v_ref[tile].astype(F32) * keep).astype(BF16)
    for copy in copies[1:]:
        copy.wait()


def unit_width(chunk, height):
    return chunk if chunk % 128 == 0 else height


def piece_count(plane, packed):
    return plane + 1 if packed else 1


def piece_start(plane, here, packed):
    before = sum(piece_count(other, packed) for other in range(plane))
    own = here + 1 if packed else 1
    return before - jnp.where(here < plane, own, 0)


def piece_total(n_col, packed):
    return sum(piece_count(plane, packed) for plane in range(1, n_col))


def join_kernel(n_col, packed, *refs):
    here = lax.axis_index("col")
    out_ref = refs[-1]
    unit = out_ref.shape[2]
    for mask in range(1, n_col):
        plane = lax.bitwise_xor(here, mask)
        value = refs[mask - 1]
        for source in range(n_col):

            @pl.when(plane == source)
            def _():
                start = piece_start(source, here, packed)
                for index in range(piece_count(source, packed)):
                    out_ref[start + index] = value[:, index * unit : (index + 1) * unit]


def eliminate(blocks):
    size = blocks[0].shape[0]
    count = size // GROUP
    unit = (
        lax.broadcasted_iota(jnp.int32, (size, size), 1)
        == lax.broadcasted_iota(jnp.int32, (size, size), 0)
    ).astype(F32)
    shape = (GROUP, 2 * size)
    sub = lax.broadcasted_iota(jnp.int32, shape, 0)
    held = []
    for block in blocks:
        both = jnp.concatenate([block, unit], axis=1)
        held.append([both[g * GROUP : (g + 1) * GROUP] for g in range(count)])

    def row_of(value, index):
        return jnp.broadcast_to(value[index : index + 1, :], shape)

    for g in range(count):
        for rows in held:
            columns = []
            for j in range(GROUP):
                spot = g * GROUP + j
                columns.append(
                    [jnp.broadcast_to(rows[h][:, spot : spot + 1], shape) for h in range(g, count)]
                )
            roots = []
            for j in range(GROUP):
                root = lax.rsqrt(row_of(columns[j][0], j))
                scaled = [value * root for value in columns[j]]
                scaled[0] = jnp.where(sub > j, scaled[0], 0.0)
                columns[j] = scaled
                roots.append(root)
                for k in range(j + 1, GROUP):
                    weight = row_of(scaled[0], k)
                    columns[k] = [a - b * weight for a, b in zip(columns[k], scaled)]
            top = rows[g]
            done = []
            for j in range(GROUP):
                row = row_of(top, j) * roots[j]
                done.append(row)
                top = jnp.where(sub == j, row, top - columns[j][0] * row)
            rows[g] = top
            for h in range(g + 1, count):
                for j in range(GROUP):
                    rows[h] = rows[h] - columns[j][h - g] * done[j]
    return [jnp.concatenate(rows, axis=0)[:, size:] for rows in held]


def block_sizes(width):
    sizes = []
    while width > 0:
        sizes.append(min(64, width))
        width -= sizes[-1]
    return sizes


def inverse_factors(grams, fillers):
    width = grams[0].shape[0]
    unit = (
        lax.broadcasted_iota(jnp.int32, (width, width), 0)
        == lax.broadcasted_iota(jnp.int32, (width, width), 1)
    ).astype(F32)
    rests = list(grams)
    sides = [unit for _ in grams]
    found = [[] for _ in grams]
    for turn, size in enumerate(block_sizes(width)):
        if turn < len(fillers):
            fillers[turn]()
        smalls = eliminate([rest[:size, :size] for rest in rests])
        for index, small in enumerate(smalls):
            rest, side = rests[index], sides[index]
            right = contract(small, side[:size], NN, HIGH)
            found[index].append(right)
            if rest.shape[0] > size:
                down = contract(rest[size:, :size], small, NT, HIGH)
                across = contract(small, rest[:size, size:], NN, HIGH)
                rests[index] = rest[size:, size:] - contract(down, across, NN, HIGH)
                sides[index] = side[size:] - contract(down, right, NN, HIGH)
    return [jnp.concatenate(rows, axis=0) for rows in found]


def six(left, right, dims):
    size, other = left.shape[0] // 3, right.shape[0] // 3
    first = contract(left, right[:other], dims)
    second = contract(left[: 2 * size], right[other : 2 * other], dims)
    third = contract(left[:size], right[2 * other :], dims)
    small = (first[2 * size :] + second[size:]) + third
    return first[:size] + ((first[size : 2 * size] + second[:size]) + small)


def three(left, right, dims):
    size, other = left.shape[0] // 2, right.shape[0] // 3
    first = contract(left, right[:other], dims)
    return first[:size] + (first[size:] + contract(left[:size], right[other : 2 * other], dims))


def spread_place(value, n_col):
    return value % 2 * (n_col // 2) + value // 2


def gather_place(value, n_col):
    return lax.rem(value, n_col // 2) * 2 + lax.div(value, n_col // 2)


def tile_kernel(n_row, n_col, columns, shares, packed, rank_ref, *refs):
    (u_ref, v_hbm, w_hbm, inverse_ref), refs = refs[:4], refs[4:]
    far, near, refs = refs[:n_row], refs[n_row : n_row + n_col], refs[n_row + n_col :]
    pieces, refs = refs[:shares], refs[shares:]
    new_u_hbm, new_v_hbm, far_ref, near_ref, full, parts_ref, *refs = refs
    new_u_ref, new_v_ref, v_ref, w_ref, out_sem, in_sem = refs
    here = (lax.axis_index("row"), lax.axis_index("col"))

    def begin(copies):
        for copy in copies:
            copy.start()
        return copies

    def end(copies):
        for copy in copies:
            copy.wait()

    loads = begin(
        [
            pltpu.make_async_copy(v_hbm, v_ref, in_sem.at[0]),
            pltpu.make_async_copy(w_hbm, w_ref, in_sem.at[1]),
        ]
    )
    for flip in range(shares):
        spot = lax.rem(lax.bitwise_xor(here[0], flip), shares)
        unit = pieces[flip].shape[2]
        for plane in range(n_col):
            start = piece_start(plane, here[1], packed)
            count = piece_count(plane, packed)

            @pl.when(here[1] != plane)
            def _():
                for index in range(count):
                    lanes = slice(index * unit, (index + 1) * unit)
                    full[plane, spot, :, lanes] = pieces[flip][start + index]

            @pl.when(here[1] == plane)
            def _():
                lanes = slice(0, count * unit)
                full[plane, spot, :, lanes] = inverse_ref[spot, :, lanes]

    for flip in range(n_row):
        source = lax.bitwise_xor(here[0], flip)
        chunk_of = lax.bitwise_xor(gather_place(lax.rem(source, n_col), n_col), here[1])
        far_ref[lax.div(source, n_col), chunk_of] = far[flip][...]
    for shift in range(n_col):
        near_ref[lax.bitwise_xor(here[1], shift)] = near[shift][...]
    width, height = u_ref.shape[3:]
    chunk = height // n_col
    spans = [slice(a * chunk, (a + 1) * chunk) for a in range(n_col)]
    eye = lax.broadcasted_iota(jnp.int32, (width, width), 0) == lax.broadcasted_iota(
        jnp.int32, (width, width), 1
    )
    across = [below(width, rank_ref[0, 0, c], 1) for c in range(columns)]

    def joined(index, c=None):
        if c is None:
            return jnp.concatenate([near_ref[a, index] for a in range(n_col)], axis=1)
        return jnp.concatenate([far_ref[c, a, index] for a in range(n_col)], axis=1)

    right = jnp.concatenate([joined(1, c) for c in range(columns)] + [joined(1)], axis=0)
    solved = []
    for a in range(n_col):
        last = (a + 1) * chunk
        piece = jnp.concatenate([full[a, share] for share in range(shares)], axis=0)
        solved.append(contract(right[:, :last], piece[:, :last], NT).astype(BF16))
    solved = jnp.concatenate(solved, axis=1)
    couplings = [
        contract(solved[columns * width :], solved[c * width : (c + 1) * width], NT)
        for c in range(columns)
    ]
    end(loads)
    far_u = [joined(0, c) for c in range(columns)]
    near_u = joined(0)
    far_parts = []
    for c in range(columns):
        right = contract(w_ref[c, 0, 0], far_u[c], NT) * below(width, rank_ref[0, 0, c], 0)
        far_parts.append(stacked(-contract(right, couplings[c], NT, HIGH), 2))
    own_parts = []
    for c in range(columns):
        rank = rank_ref[0, 0, c]
        value = contract(w_ref[c, 0, 0], v_ref[c, 0, 0], NT)
        own_parts.append(stacked(value * below(width, rank, 0) * across[c], 2))
    for c in range(columns):
        for a in range(n_col):
            y = folded(
                contract(own_parts[c], u_ref[c, 0, 0, :, spans[a]], NN)
                + contract(far_parts[c], near_ref[a, 0], NN),
                2,
            )
            parts_ref[c, a] = stacked(y, 3)
    grams = []
    for c in range(columns):
        y = jnp.concatenate([parts_ref[c, a] for a in range(n_col)], axis=1)
        grams.append(six(y, y, NT) + jnp.where(eye, 1.0 - across[c], 0.0))
    own, far = [None] * columns, [None] * columns

    def project(c):
        y = jnp.concatenate([parts_ref[c, a] for a in range(n_col)], axis=1)
        own[c] = folded(contract(y, u_ref[c, 0, 0], NT), 3) * across[c]
        far[c] = folded(contract(y, near_u, NT), 3)

    inverses = inverse_factors(grams, [functools.partial(project, c) for c in range(columns)])
    factor = math.sqrt(height)
    sides = []
    for c in range(columns):
        scaled = inverses[c] * (1.0 / factor)
        left = contract(scaled, own[c], NN, HIGH)
        right = contract(contract(scaled, -far[c], NN, HIGH), couplings[c], NN, HIGH)
        sides.append((stacked(left, 2), stacked(right, 2)))
    outs = []
    reach = max(1, OUT_LANES // chunk)

    def send(index, c, a, room, target):
        if (a + 1) % reach == 0:
            lanes = slice((a + 1 - reach) * chunk, (a + 1) * chunk)
            spot = (c, 0, 0, slice(None), lanes)
            copy = pltpu.make_async_copy(room.at[spot], target.at[spot], out_sem.at[index, c, a])
            outs.extend(begin([copy]))

    for c in range(columns):
        scaled = stacked(inverses[c] * factor, 2)
        for a in range(n_col):
            new_u_ref[c, 0, 0, :, spans[a]] = three(scaled, parts_ref[c, a], NN)
            send(0, c, a, new_u_ref, new_u_hbm)
    for c in range(columns):
        left, right = sides[c]
        for a in range(n_col):
            new_v_ref[c, 0, 0, :, spans[a]] = folded(
                contract(left, v_ref[c, 0, 0, :, spans[a]], NN)
                + contract(right, far_ref[c, a, 0], NN),
                2,
            )
            send(1, c, a, new_v_ref, new_v_hbm)
    end(outs)


def in_hbm(value):
    return pltpu.with_memory_space_constraint(value, pltpu.HBM)


def share_count(n_row, chunk):
    return max(1, min(n_row, chunk // SHARE_ROWS))


def whole(panel_u, panel_v, panel_rank, diag_inverse, tile_u, tile_v, tile_rank, sketch):
    n_row, n_col = lax.axis_size("row"), lax.axis_size("col")
    panel_u, panel_v, tile_u, tile_v, sketch = (
        jnp.swapaxes(value, -1, -2) for value in (panel_u, panel_v, tile_u, tile_v, sketch)
    )
    panel_rank, tile_rank = jnp.swapaxes(panel_rank, 0, 1), jnp.moveaxis(tile_rank, 0, -1)
    width, chunk = panel_u.shape[2:]
    columns = tile_u.shape[0]
    pair = jax.ShapeDtypeStruct((2, width, chunk), BF16)

    def across(value):
        pairs = []
        for row in range(n_row):
            for col in range(n_col):
                spot = spread_place(row % n_col ^ col, n_col)
                pairs.append((row * n_col + col, (row // n_col * n_col + spot) * n_col + row % n_col))
        return lax.ppermute(value, ("row", "col"), pairs)

    def flip(value, mask):
        return lax.ppermute(value, "row", [(i, i ^ mask) for i in range(n_row)])

    def plane(value, count):
        same = {0: value}
        for mask in range(2, count, 2):
            same[mask] = flip(value, mask)
        full = dict(same)
        for mask in range(0, count, 2):
            full[mask + 1] = flip(same[mask], 1)
        return [full[mask] for mask in range(count)]

    def along(value):
        found = [value]
        for shift in range(1, n_col):
            pairs = [(i, i ^ shift) for i in range(n_col)]
            found.append(lax.ppermute(value, "col", pairs))
        return found

    shares = share_count(n_row, chunk)
    part = jax.ShapeDtypeStruct((chunk // shares, diag_inverse.shape[1]), BF16)
    unit = unit_width(chunk, diag_inverse.shape[1])
    packed = unit == chunk
    total = piece_total(n_col, packed)
    far, near, share = pl.pallas_call(
        functools.partial(pack_kernel, shares),
        out_shape=(pair, pair, part),
        in_specs=[SMEM] + [HBM] * 3,
        out_specs=(VMEM,) * 3,
        scratch_shapes=[
            pltpu.VMEM((2, width, chunk), BF16),
            pltpu.SemaphoreType.DMA((4,)),
        ],
        compiler_params=LIGHT,
        name="pack",
    )(*(in_hbm(value) for value in (panel_rank, panel_u, panel_v, diag_inverse)))
    far, shared = across(far), along(share)[1:]
    near, far = along(near), plane(far, n_row)
    joined = pl.pallas_call(
        functools.partial(join_kernel, n_col, packed),
        out_shape=jax.ShapeDtypeStruct((total, share.shape[0], unit), BF16),
        in_specs=[VMEM] * (n_col - 1),
        out_specs=VMEM,
        compiler_params=LIGHT,
        name="join",
    )(*shared)
    pieces = plane(joined, shares)
    result = jax.ShapeDtypeStruct(tile_u.shape, F32)
    new_u, new_v = pl.pallas_call(
        functools.partial(tile_kernel, n_row, n_col, columns, shares, packed),
        out_shape=(result, result),
        in_specs=[SMEM, VMEM, HBM, HBM] + [VMEM] * (1 + n_row + n_col + shares),
        out_specs=(HBM, HBM),
        scratch_shapes=[
            pltpu.VMEM((columns, n_col, 2, width, chunk), BF16),
            pltpu.VMEM((n_col, 2, width, chunk), BF16),
            pltpu.VMEM((n_col, shares) + share.shape, BF16),
            pltpu.VMEM((columns, n_col, 3 * width, chunk), BF16),
            *[pltpu.VMEM(tile_u.shape, F32)] * 2,
            *[pltpu.VMEM(tile_u.shape, BF16)] * 2,
            pltpu.SemaphoreType.DMA((2, columns, n_col)),
            pltpu.SemaphoreType.DMA((2,)),
        ],
        compiler_params=pltpu.CompilerParams(vmem_limit_bytes=22 * MIB),
        name="tiles",
    )(in_hbm(tile_rank), tile_u, in_hbm(tile_v), in_hbm(sketch), diag_inverse.reshape((shares,) + share.shape), *far, *near, *pieces)
    return jnp.swapaxes(new_u, -1, -2), jnp.swapaxes(new_v, -1, -2)


def solution(mesh):
    n_row, n_col = mesh.shape["row"], mesh.shape["col"]
    assert n_row % n_col == 0
    wide = P(None, "row", "col", None)
    tile = P(None, "row", "col", None, None)
    return jax.shard_map(
        whole,
        mesh=mesh,
        in_specs=(wide, wide, P(None, "row"), P("col", None), tile, tile, P(None, "row", "col"), tile),
        out_specs=(tile, tile),
        check_vma=False,
    )
```

```python
import functools
import math

import jax
import jax.numpy as jnp
from jax import lax
from jax.experimental import pallas as pl
from jax.experimental.pallas import tpu as pltpu
from jax.sharding import PartitionSpec as P


F32 = jnp.float32
BF16 = jnp.bfloat16
HIGH = lax.Precision.HIGHEST
GROUP = 8
SHARE_ROWS = 32
OUT_LANES = 256
VMEM = pl.BlockSpec(memory_space=pltpu.VMEM)
SMEM = pl.BlockSpec(memory_space=pltpu.SMEM)
HBM = pl.BlockSpec(memory_space=pltpu.HBM)
MIB = 1024 * 1024
LIGHT = pltpu.CompilerParams(vmem_limit_bytes=6 * MIB)

NN = ((1,), (0,))
NT = ((1,), (1,))


def contract(a, b, dims, precision=None):
    return lax.dot_general(
        a, b, (dims, ((), ())), preferred_element_type=F32, precision=precision
    )


def split(value, count):
    found = []
    for _ in range(count - 1):
        found.append(value.astype(BF16))
        value = value - found[-1].astype(F32)
    return found + [value.astype(BF16)]


def stacked(value, count):
    return jnp.concatenate(split(value, count), axis=0)


def beside(*values):
    return jnp.concatenate(values, axis=1)


def product(left, *rights):
    return contract(left, jnp.concatenate(rights, axis=0), NN)


def folded(value, count):
    size = value.shape[0] // count
    total = value[(count - 1) * size :]
    for index in range(count - 2, -1, -1):
        total = value[index * size : (index + 1) * size] + total
    return total


def below(width, rank, axis):
    shape = (width, 1) if axis == 0 else (1, width)
    return (lax.broadcasted_iota(jnp.int32, shape, axis) < rank).astype(F32)


def pack_kernel(shares, rank_ref, u_hbm, v_hbm, inverse_hbm, far_ref, near_ref, share_ref, v_ref, sem):
    rows, width = share_ref.shape[0], v_ref.shape[1]
    start = lax.rem(lax.axis_index("row"), shares) * rows
    part = inverse_hbm.at[pl.ds(pl.multiple_of(start, rows), rows), :]
    copies = [
        pltpu.make_async_copy(v_hbm.at[:, 0], v_ref, sem.at[0]),
        pltpu.make_async_copy(part, share_ref, sem.at[1]),
        pltpu.make_async_copy(u_hbm.at[0, 0], far_ref.at[0], sem.at[2]),
        pltpu.make_async_copy(u_hbm.at[1, 0], near_ref.at[0], sem.at[3]),
    ]
    for copy in copies:
        copy.start()
    copies[0].wait()
    for tile, out_ref in enumerate((far_ref, near_ref)):
        keep = below(width, rank_ref[0, tile], 0)
        out_ref[1] = (v_ref[tile].astype(F32) * keep).astype(BF16)
    for copy in copies[1:]:
        copy.wait()


def unit_width(chunk, height):
    return chunk if chunk % 128 == 0 else height


def piece_count(plane, packed):
    return plane + 1 if packed else 1


def piece_starts(own, n_col, packed):
    starts, total = [], 0
    for plane in range(n_col):
        starts.append(total)
        total += 0 if plane == own else piece_count(plane, packed)
    return starts


def piece_total(n_col, packed):
    return sum(piece_count(plane, packed) for plane in range(1, n_col))


def join_kernel(n_col, packed, *refs):
    out_ref = refs[-1]
    unit = out_ref.shape[2]

    def pack(own):
        starts = piece_starts(own, n_col, packed)
        for mask in range(1, n_col):
            for index in range(piece_count(own ^ mask, packed)):
                lanes = slice(index * unit, (index + 1) * unit)
                out_ref[starts[own ^ mask] + index] = refs[mask - 1][:, lanes]

    for own in range(n_col):
        pl.when(lax.axis_index("col") == own)(functools.partial(pack, own))


def eliminate(blocks):
    size = blocks[0].shape[0]
    count = size // GROUP
    unit = (
        lax.broadcasted_iota(jnp.int32, (size, size), 1)
        == lax.broadcasted_iota(jnp.int32, (size, size), 0)
    ).astype(F32)
    both = jnp.concatenate([part for block in blocks for part in (block, unit)], axis=1)
    shape = (GROUP, both.shape[1])
    sub = lax.broadcasted_iota(jnp.int32, shape, 0)
    lane = lax.broadcasted_iota(jnp.int32, shape, 1)
    rows = [both[g * GROUP : (g + 1) * GROUP] for g in range(count)]

    def row_of(value, index):
        return jnp.broadcast_to(value[index : index + 1, :], shape)

    def column_of(value, index):
        found = jnp.broadcast_to(value[:, index : index + 1], shape)
        for turn in range(1, len(blocks)):
            spot = 2 * size * turn + index
            found = jnp.where(
                lane < 2 * size * turn, found, jnp.broadcast_to(value[:, spot : spot + 1], shape)
            )
        return found

    for g in range(count):
        columns = [
            [column_of(rows[h], g * GROUP + j) for h in range(g, count)] for j in range(GROUP)
        ]
        roots = []
        for j in range(GROUP):
            root = lax.rsqrt(row_of(columns[j][0], j))
            scaled = [value * root for value in columns[j]]
            scaled[0] = jnp.where(sub > j, scaled[0], 0.0)
            columns[j] = scaled
            roots.append(root)
            for k in range(j + 1, GROUP):
                weight = row_of(scaled[0], k)
                columns[k] = [a - b * weight for a, b in zip(columns[k], scaled)]
        top = rows[g]
        done = []
        for j in range(GROUP):
            row = row_of(top, j) * roots[j]
            done.append(row)
            top = jnp.where(sub == j, row, top - columns[j][0] * row)
        rows[g] = top
        for h in range(g + 1, count):
            for j in range(GROUP):
                rows[h] = rows[h] - columns[j][h - g] * done[j]
    whole = jnp.concatenate(rows, axis=0)
    return [
        whole[:, (2 * turn + 1) * size : (2 * turn + 2) * size] for turn in range(len(blocks))
    ]


def block_sizes(width):
    sizes = []
    while width > 0:
        sizes.append(min(64, width))
        width -= sizes[-1]
    return sizes


def inverse_factors(grams, fillers):
    width = grams[0].shape[0]
    unit = (
        lax.broadcasted_iota(jnp.int32, (width, width), 0)
        == lax.broadcasted_iota(jnp.int32, (width, width), 1)
    ).astype(F32)
    rests = list(grams)
    sides = [unit for _ in grams]
    found = [[] for _ in grams]
    for turn, size in enumerate(block_sizes(width)):
        if turn < len(fillers):
            fillers[turn]()
        smalls = eliminate([rest[:size, :size] for rest in rests])
        for index, small in enumerate(smalls):
            rest, side = rests[index], sides[index]
            right = contract(small, side[:size], NN, HIGH)
            found[index].append(right)
            if rest.shape[0] > size:
                down = contract(rest[size:, :size], small, NT, HIGH)
                across = contract(small, rest[:size, size:], NN, HIGH)
                rests[index] = rest[size:, size:] - contract(down, across, NN, HIGH)
                sides[index] = side[size:] - contract(down, right, NN, HIGH)
    return [jnp.concatenate(rows, axis=0) for rows in found]


def six(left, right, dims):
    size, other = left.shape[0] // 3, right.shape[0] // 3
    first = contract(left, right[:other], dims)
    second = contract(left[: 2 * size], right[other : 2 * other], dims)
    third = contract(left[:size], right[2 * other :], dims)
    small = (first[2 * size :] + second[size:]) + third
    return first[:size] + ((first[size : 2 * size] + second[:size]) + small)


def spread_place(value, n_col):
    return value % 2 * (n_col // 2) + value // 2


def gather_place(value, n_col):
    return lax.rem(value, n_col // 2) * 2 + lax.div(value, n_col // 2)


def tile_kernel(n_row, n_col, columns, shares, packed, rank_ref, *refs):
    (u_ref, v_hbm, w_hbm, inverse_ref), refs = refs[:4], refs[4:]
    far, near, refs = refs[:n_row], refs[n_row : n_row + n_col], refs[n_row + n_col :]
    pieces, refs = refs[:shares], refs[shares:]
    new_u_hbm, new_v_hbm, far_ref, near_ref, full, parts_ref, *refs = refs
    new_u_ref, new_v_ref, v_ref, w_ref, out_sem, in_sem = refs
    here = (lax.axis_index("row"), lax.axis_index("col"))

    def begin(copies):
        for copy in copies:
            copy.start()
        return copies

    def end(copies):
        for copy in copies:
            copy.wait()

    loads = begin(
        [
            pltpu.make_async_copy(v_hbm, v_ref, in_sem.at[0]),
            pltpu.make_async_copy(w_hbm, w_ref, in_sem.at[1]),
        ]
    )
    unit = pieces[0].shape[2]

    def unpack(own):
        starts = piece_starts(own, n_col, packed)
        for flip in range(shares):
            spot = lax.rem(lax.bitwise_xor(here[0], flip), shares)
            for plane in range(n_col):
                for index in range(piece_count(plane, packed)):
                    lanes = slice(index * unit, (index + 1) * unit)
                    if plane == own:
                        full[plane, spot, :, lanes] = inverse_ref[spot, :, lanes]
                    else:
                        full[plane, spot, :, lanes] = pieces[flip][starts[plane] + index]

    for own in range(n_col):
        pl.when(here[1] == own)(functools.partial(unpack, own))
    for flip in range(n_row):
        source = lax.bitwise_xor(here[0], flip)
        chunk_of = lax.bitwise_xor(gather_place(lax.rem(source, n_col), n_col), here[1])
        far_ref[lax.div(source, n_col), chunk_of] = far[flip][...]
    for shift in range(n_col):
        near_ref[lax.bitwise_xor(here[1], shift)] = near[shift][...]
    width, height = u_ref.shape[3:]
    chunk = height // n_col
    spans = [slice(a * chunk, (a + 1) * chunk) for a in range(n_col)]
    eye = lax.broadcasted_iota(jnp.int32, (width, width), 0) == lax.broadcasted_iota(
        jnp.int32, (width, width), 1
    )
    across = [below(width, rank_ref[0, 0, c], 1) for c in range(columns)]

    def joined(index, c=None):
        if c is None:
            return jnp.concatenate([near_ref[a, index] for a in range(n_col)], axis=1)
        return jnp.concatenate([far_ref[c, a, index] for a in range(n_col)], axis=1)

    right = jnp.concatenate([joined(1, c) for c in range(columns)] + [joined(1)], axis=0)
    solved = []
    for a in range(n_col):
        last = (a + 1) * chunk
        piece = jnp.concatenate([full[a, share] for share in range(shares)], axis=0)
        solved.append(contract(right[:, :last], piece[:, :last], NT).astype(BF16))
    solved = jnp.concatenate(solved, axis=1)
    couplings = [
        contract(solved[columns * width :], solved[c * width : (c + 1) * width], NT)
        for c in range(columns)
    ]
    end(loads)
    far_u = [joined(0, c) for c in range(columns)]
    near_u = joined(0)
    far_parts = []
    for c in range(columns):
        right = contract(w_ref[c, 0, 0], far_u[c], NT) * below(width, rank_ref[0, 0, c], 0)
        far_parts.append(split(-contract(right, couplings[c], NT, HIGH), 2))
    own_parts = []
    for c in range(columns):
        rank = rank_ref[0, 0, c]
        value = contract(w_ref[c, 0, 0], v_ref[c, 0, 0], NT)
        own_parts.append(split(value * below(width, rank, 0) * across[c], 2))
    for c in range(columns):
        left = beside(*own_parts[c], *far_parts[c])
        for a in range(n_col):
            own, far = u_ref[c, 0, 0, :, spans[a]], near_ref[a, 0]
            y = product(left, own, own, far, far)
            parts_ref[c, a] = stacked(y, 3)
    grams = []
    for c in range(columns):
        y = jnp.concatenate([parts_ref[c, a] for a in range(n_col)], axis=1)
        grams.append(six(y, y, NT) + jnp.where(eye, 1.0 - across[c], 0.0))
    own, far = [None] * columns, [None] * columns

    def project(c):
        y = jnp.concatenate([parts_ref[c, a] for a in range(n_col)], axis=1)
        own[c] = folded(contract(y, u_ref[c, 0, 0], NT), 3) * across[c]
        far[c] = folded(contract(y, near_u, NT), 3)

    inverses = inverse_factors(grams, [functools.partial(project, c) for c in range(columns)])
    factor = math.sqrt(height)
    sides = []
    for c in range(columns):
        scaled = inverses[c] * (1.0 / factor)
        left = contract(scaled, own[c], NN, HIGH)
        right = contract(contract(scaled, -far[c], NN, HIGH), couplings[c], NN, HIGH)
        sides.append(beside(*split(left, 2), *split(right, 2)))
    outs = []
    reach = max(1, OUT_LANES // chunk)

    def send(index, c, a, room, target):
        if (a + 1) % reach == 0:
            lanes = slice((a + 1 - reach) * chunk, (a + 1) * chunk)
            spot = (c, 0, 0, slice(None), lanes)
            copy = pltpu.make_async_copy(room.at[spot], target.at[spot], out_sem.at[index, c, a])
            outs.extend(begin([copy]))

    for c in range(columns):
        head, tail = split(inverses[c] * factor, 2)
        scaled = beside(tail, head, head)
        for a in range(n_col):
            head, middle = parts_ref[c, a, :width], parts_ref[c, a, width : 2 * width]
            new_u_ref[c, 0, 0, :, spans[a]] = product(scaled, head, head, middle)
            send(0, c, a, new_u_ref, new_u_hbm)
    for c in range(columns):
        for a in range(n_col):
            own, far = v_ref[c, 0, 0, :, spans[a]], far_ref[c, a, 0]
            new_v_ref[c, 0, 0, :, spans[a]] = product(sides[c], own, own, far, far)
            send(1, c, a, new_v_ref, new_v_hbm)
    end(outs)


def in_hbm(value):
    return pltpu.with_memory_space_constraint(value, pltpu.HBM)


def share_count(n_row, chunk):
    return max(1, min(n_row, chunk // SHARE_ROWS))


def whole(panel_u, panel_v, panel_rank, diag_inverse, tile_u, tile_v, tile_rank, sketch):
    n_row, n_col = lax.axis_size("row"), lax.axis_size("col")
    panel_u, panel_v, tile_u, tile_v, sketch = (
        jnp.swapaxes(value, -1, -2) for value in (panel_u, panel_v, tile_u, tile_v, sketch)
    )
    panel_rank, tile_rank = jnp.swapaxes(panel_rank, 0, 1), jnp.moveaxis(tile_rank, 0, -1)
    width, chunk = panel_u.shape[2:]
    columns = tile_u.shape[0]
    pair = jax.ShapeDtypeStruct((2, width, chunk), BF16)

    def across(value):
        pairs = []
        for row in range(n_row):
            for col in range(n_col):
                spot = spread_place(row % n_col ^ col, n_col)
                pairs.append((row * n_col + col, (row // n_col * n_col + spot) * n_col + row % n_col))
        return lax.ppermute(value, ("row", "col"), pairs)

    def flip(value, mask):
        return lax.ppermute(value, "row", [(i, i ^ mask) for i in range(n_row)])

    def plane(value, count):
        same = {0: value}
        for mask in range(2, count, 2):
            same[mask] = flip(value, mask)
        full = dict(same)
        for mask in range(0, count, 2):
            full[mask + 1] = flip(same[mask], 1)
        return [full[mask] for mask in range(count)]

    def along(value):
        found = [value]
        for shift in range(1, n_col):
            pairs = [(i, i ^ shift) for i in range(n_col)]
            found.append(lax.ppermute(value, "col", pairs))
        return found

    shares = share_count(n_row, chunk)
    part = jax.ShapeDtypeStruct((chunk // shares, diag_inverse.shape[1]), BF16)
    unit = unit_width(chunk, diag_inverse.shape[1])
    packed = unit == chunk
    total = piece_total(n_col, packed)
    far, near, share = pl.pallas_call(
        functools.partial(pack_kernel, shares),
        out_shape=(pair, pair, part),
        in_specs=[SMEM] + [HBM] * 3,
        out_specs=(VMEM,) * 3,
        scratch_shapes=[
            pltpu.VMEM((2, width, chunk), BF16),
            pltpu.SemaphoreType.DMA((4,)),
        ],
        compiler_params=LIGHT,
        name="pack",
    )(*(in_hbm(value) for value in (panel_rank, panel_u, panel_v, diag_inverse)))
    far, shared = across(far), along(share)[1:]
    near, far = along(near), plane(far, n_row)
    joined = pl.pallas_call(
        functools.partial(join_kernel, n_col, packed),
        out_shape=jax.ShapeDtypeStruct((total, share.shape[0], unit), BF16),
        in_specs=[VMEM] * (n_col - 1),
        out_specs=VMEM,
        compiler_params=LIGHT,
        name="join",
    )(*shared)
    pieces = plane(joined, shares)
    result = jax.ShapeDtypeStruct(tile_u.shape, F32)
    new_u, new_v = pl.pallas_call(
        functools.partial(tile_kernel, n_row, n_col, columns, shares, packed),
        out_shape=(result, result),
        in_specs=[SMEM, VMEM, HBM, HBM] + [VMEM] * (1 + n_row + n_col + shares),
        out_specs=(HBM, HBM),
        scratch_shapes=[
            pltpu.VMEM((columns, n_col, 2, width, chunk), BF16),
            pltpu.VMEM((n_col, 2, width, chunk), BF16),
            pltpu.VMEM((n_col, shares) + share.shape, BF16),
            pltpu.VMEM((columns, n_col, 3 * width, chunk), BF16),
            *[pltpu.VMEM(tile_u.shape, F32)] * 2,
            *[pltpu.VMEM(tile_u.shape, BF16)] * 2,
            pltpu.SemaphoreType.DMA((2, columns, n_col)),
            pltpu.SemaphoreType.DMA((2,)),
        ],
        compiler_params=pltpu.CompilerParams(vmem_limit_bytes=22 * MIB),
        name="tiles",
    )(in_hbm(tile_rank), tile_u, in_hbm(tile_v), in_hbm(sketch), diag_inverse.reshape((shares,) + share.shape), *far, *near, *pieces)
    return jnp.swapaxes(new_u, -1, -2), jnp.swapaxes(new_v, -1, -2)


def solution(mesh):
    n_row, n_col = mesh.shape["row"], mesh.shape["col"]
    assert n_row % n_col == 0
    wide = P(None, "row", "col", None)
    tile = P(None, "row", "col", None, None)
    return jax.shard_map(
        whole,
        mesh=mesh,
        in_specs=(wide, wide, P(None, "row"), P("col", None), tile, tile, P(None, "row", "col"), tile),
        out_specs=(tile, tile),
        check_vma=False,
    )
```
